512 devices in a mesh: tm: 16 (over z, core), space: 32 (over y, x).
Axes of the slice: x: 4, y: 8, z: 8, core: 2. Of those that a mesh axis runs over, the one named last changes fastest.
Arguments:
- increments: float32 [16, 8, 256, 1440], P('tm', None, 'space'), may hold values from -6 to 6
- background: float32 [8, 256, 1440], P(None, 'space'), may hold values from -6 to 6
- error_weight: float32 [8, 256, 1440], P(None, 'space'), may hold values from 0.5 to 2
- neighbor_weights: float32 [4, 256, 1440], P(None, 'space'), may hold values from 0.03 to 0.24
- operators: bfloat16 [16, 4, 768, 128, 128], P('tm', None, 'space'), may hold values from -0.5 to 0.5
- values: float32 [16, 4, 768, 128], P('tm', None, 'space'), may hold values from -6 to 6
- obs_weight: float32 [16, 4, 768, 128], P('tm', None, 'space'), may hold values from 0.3 to 3
- owners: int32 [16, 4, 768, 1], P('tm', None, 'space'), may hold values from 0 to 31; in each aligned block of 24 rows (0 to 23, 24 to 47, ..., all dimensions but the last counted through in order) at most 2 rows name the same one
- columns: int32 [16, 4, 768], P('tm', None, 'space'), may hold values from 0 to 719
Outputs:
- gradient: float32 [16, 8, 256, 1440], P('tm', None, 'space')
- departures: float32 [16, 4, 768, 128], P('tm', None, 'space')
The draws below stay inside these ranges and needn't reach their ends.
Inputs may be any that keep to these rules, and one draw needn't show every extreme that they name: `owners`: among the 24 observation blocks of one step that one slab holds, at most 2 name the same owner slab, and in some such groups exactly 2 do.
All inputs are finite; a program needn't handle non-finite values.
Results may differ from the reference program's by a relative error of at most 0.003.
Values may be sent and summed in bfloat16 or wider, within the bound.
No kernel may reach another device: no remote copies, remote signals or barrier semaphores. Data moves between devices by JAX's collectives and lax.ppermute only.
A program may use at most 64 MiB of HBM per device.

```python
import math
import jax
import jax.numpy as jnp
import numpy as np
from jax import lax

LON = 1440
LEV = 8
LAT_DEV = 8
STEPS = 4
BLK = 128
OBS_DEV = 24
CAP = 2
BLOCKS = 720
LAT = 256
OBS = 768
WINDOWS = 16
N_SPACE = 32


def place_ends(entries, own_key, low, high):
    shape = entries.shape
    place = [jax.random.randint(jax.random.fold_in(own_key, axis), (), 0, shape[axis]) for axis in range(len(shape))]
    entries = entries.at[tuple(place)].set(low)
    longest = shape.index(max(shape))
    place[longest] = (place[longest] + 1) % shape[longest]
    return entries.at[tuple(place)].set(high)


def level_of(stream_key, shape, pieces, smallest, top_value):
    factor_of, own = 1.0, jax.random.fold_in(stream_key, 6)
    for axis_at, parts in pieces:
        heights = jnp.exp(jax.random.uniform(jax.random.fold_in(own, axis_at), (parts,), jnp.float32, smallest / len(pieces), top_value / len(pieces)))
        factor_of = factor_of * jnp.repeat(heights, shape[axis_at] // parts).reshape([-1 if axis == axis_at else 1 for axis in range(len(shape))])
    return factor_of


def shared_out(stream_key, own, number, rows, amount, top, limit, slope):
    ranking = jax.random.permutation(stream_key, amount)
    packed, ordinary = load_shares(amount, rows * top, limit, slope, True), load_shares(amount, rows * top, limit, slope, False)
    places = jnp.arange(amount)

    def named(sizes, rotation):
        used = int((sizes > 0).sum())
        fixed = max(1, used // 4)
        moved = fixed + (places - fixed + rotation * (used - fixed)) % max(1, amount - fixed)
        return jnp.zeros((amount,), jnp.int32).at[ranking[jnp.where(places < fixed, places, moved)]].set(jnp.asarray(sizes, jnp.int32))

    sizes = jnp.where(number % 4 == 0, named(packed, number // 4), named(ordinary, number - number // 4 - 1))
    mixed = jax.random.permutation(jax.random.fold_in(own, 3), amount)
    donor, taker = mixed[0:amount // 2 * 2:2], mixed[1:amount // 2 * 2:2]
    slack = jnp.minimum(sizes[donor] - 1, limit - sizes[taker]) // 2
    slack = jnp.where((donor == ranking[0]) | (taker == ranking[0]) | (sizes[taker] == 0), 0, jnp.maximum(slack, 0))
    moved = jax.random.randint(jax.random.fold_in(own, 4), (amount // 2,), 0, 1 << 20) % (slack + 1)
    sizes = sizes.at[donor].add(-moved).at[taker].add(moved)
    labels = jnp.searchsorted(jnp.cumsum(sizes), jnp.arange(rows * top), side="right").astype(jnp.int32)
    grid = labels.reshape(top, rows).T
    grid = grid[jax.random.permutation(jax.random.fold_in(own, 1), rows)]
    rotation = jax.random.randint(jax.random.fold_in(own, 2), (rows, 1), 0, top)
    return jnp.take_along_axis(grid, (jnp.arange(top)[None, :] + rotation) % top, axis=1)


def load_shares(number_of, total, bound, slope, full):
    weights = [(1 << 20) // math.isqrt(rank ** slope) + 1 for rank in range(1, number_of + 1)]
    largest = bound if full else min(bound, max(-(-total // number_of), total * weights[0] // sum(weights)))
    least = 1 if total - largest >= number_of - 1 else 0
    holding, rest = [largest] + [least] * (number_of - 1), total - largest - least * (number_of - 1)
    while rest > 0:
        free = [i for i in range(1, number_of) if holding[i] < largest] or [i for i in range(1, number_of) if holding[i] < bound]
        mass, left = sum([weights[i] for i in free]), rest
        for i in free:
            addition = min(bound - holding[i], max(1, left * weights[i] // mass), rest)
            holding[i] = holding[i] + addition
            rest = rest - addition
    return np.array(holding)


def scatter_about(rng, extent, width, most, cuts=(), kind=jnp.bfloat16):
    values = width * jax.random.normal(rng, extent, jnp.float32)
    if cuts:
        values = values * level_of(rng, extent, cuts, -0.22, 0.18)
    return jnp.clip(values, -most, most).astype(kind)


def setup_inputs(seed: int = 0) -> dict:
    key_list = jax.random.split(jax.random.key(seed), 10)
    increments = scatter_about(key_list[0], (WINDOWS, LEV, LAT, LON), 1.0, 6.0, ((0, 16), (2, 32)), jnp.float32)
    background = scatter_about(key_list[1], (LEV, LAT, LON), 1.0, 6.0, ((1, 32),), jnp.float32)
    error_weight = jnp.clip(jnp.exp(math.log(2.0) - 1.3862944 * jax.random.uniform(key_list[2], (LEV, LAT, LON), jnp.float32) ** level_of(key_list[2], (LEV, LAT, LON), ((1, 32),), -0.2, 0.2)), 0.5, 2.0)
    neighbor_weights = jnp.clip(jnp.exp(math.log(0.24) - 2.0794415 * jax.random.uniform(key_list[3], (4, LAT, LON), jnp.float32) ** level_of(key_list[3], (4, LAT, LON), ((1, 32),), -0.2, 0.2)), 0.03, 0.24)
    operators = scatter_about(key_list[4], (WINDOWS, STEPS, OBS, BLK, BLK), BLK ** -0.5, 0.5, ((0, 16), (2, 32)))
    values = scatter_about(key_list[5], (WINDOWS, STEPS, OBS, BLK), 1.0, 6.0, ((0, 16), (2, 32)), jnp.float32)
    obs_weight = jnp.clip(jnp.exp(math.log(3.0) - 2.3025851 * jax.random.uniform(key_list[6], (WINDOWS, STEPS, OBS, BLK), jnp.float32) ** level_of(key_list[6], (WINDOWS, STEPS, OBS, BLK), ((0, 16), (2, 32)), -0.2, 0.2)), 0.3, 3.0)
    owners_keys = jax.random.split(jax.random.fold_in(key_list[7], 1), WINDOWS * STEPS * OBS // OBS_DEV)
    owners_turns = jax.random.permutation(jax.random.fold_in(key_list[7], 3), WINDOWS * STEPS * OBS // OBS_DEV)
    owners = jax.vmap(lambda own, number: shared_out(jax.random.fold_in(key_list[7], 2), own, number, OBS_DEV, N_SPACE, 1, CAP, 2))(owners_keys, owners_turns).reshape((WINDOWS, STEPS, OBS, 1))
    columns = place_ends(jax.random.randint(key_list[8], (WINDOWS, STEPS, OBS), 0, BLOCKS), jax.random.fold_in(key_list[8], 1), 0, BLOCKS - 1).astype(jnp.int32)
    return dict(increments=increments, background=background, error_weight=error_weight, neighbor_weights=neighbor_weights, operators=operators, values=values, obs_weight=obs_weight, owners=owners, columns=columns)


def forward(field, coeffs):
    east, west, north, south = (coeffs[0], coeffs[1], coeffs[2], coeffs[3])
    center = 1.0 - (east + west + north + south)
    widths = [(0, 0)] * (field.ndim - 2) + [(1, 1), (0, 0)]
    padded = jnp.pad(field, widths)
    return center * field + east * jnp.roll(field, -1, -1) + west * jnp.roll(field, 1, -1) + north * padded[..., 2:, :] + south * padded[..., :-2, :]

def to_blocks(field):
    shaped = field.reshape(WINDOWS, LEV, N_SPACE, LAT_DEV, LON).transpose(0, 2, 1, 3, 4)
    return shaped.reshape(WINDOWS, N_SPACE, BLOCKS, BLK)

def from_blocks(blocks):
    shaped = blocks.reshape(WINDOWS, N_SPACE, LEV, LAT_DEV, LON).transpose(0, 2, 1, 3, 4)
    return shaped.reshape(WINDOWS, LEV, LAT, LON)

def reference(increments, background, error_weight, neighbor_weights, operators, values, obs_weight, owners, columns):
    coeffs = neighbor_weights
    field = increments
    states = []
    for step in range(STEPS):
        field = forward(field, coeffs)
        states.append(field)
    start = jnp.concatenate([background[None], field[:-1]], 0)
    weighted = error_weight[None] * (increments - start)
    adjoint = -jnp.concatenate([weighted[1:], jnp.zeros_like(weighted[:1])], 0)
    windows = jnp.arange(WINDOWS, dtype=jnp.int32)[:, None]
    forcing = []
    departures = []
    for step in range(STEPS):
        owner_rows = owners[:, step, :, 0]
        column_rows = columns[:, step]
        blocks = to_blocks(states[step])[windows, owner_rows, column_rows].astype(jnp.bfloat16)
        ops = operators[:, step].astype(jnp.float32)
        departure = jnp.einsum('woab,wob->woa', ops, blocks.astype(jnp.float32), precision=lax.Precision.HIGHEST) - values[:, step]
        departures.append(departure)
        scaled = lax.optimization_barrier((obs_weight[:, step] * departure).astype(jnp.bfloat16)).astype(jnp.float32)
        increment = jnp.einsum('woab,woa->wob', ops, scaled, precision=lax.Precision.HIGHEST)
        target = jnp.zeros((WINDOWS, N_SPACE, BLOCKS, BLK), jnp.float32)
        target = target.at[windows, owner_rows, column_rows].add(increment)
        forcing.append(from_blocks(target))
    for step in range(STEPS - 1, -1, -1):
        adjoint = adjoint + forcing[step]
        pulled = jax.vjp(lambda v: forward(v, coeffs), adjoint)[1]
        adjoint = pulled(adjoint)[0]
    gradient = weighted + adjoint
    return (gradient, jnp.stack(departures, 1))
```

```python
import jax
import jax.numpy as jnp
from jax import lax
from jax.experimental import pallas as pl
from jax.experimental.pallas import tpu as pltpu
from jax.sharding import PartitionSpec as P

LEV = 8
ROWS = 8
LON = 1440
WIDE = 1536
PAD = 48
STEPS = 4
HALO = 4
EXT = ROWS + 2 * HALO
OBS = 24
ALL_OBS = STEPS * OBS
BLK = 128
PARTS = 32
SLOTS = 2 * STEPS
SENT = 3 * SLOTS
HALF = 45
BLOCKS = 2 * HALF * LEV
F32 = jnp.float32
BF16 = jnp.bfloat16
I32 = jnp.int32


def iota(shape, dim):
    return lax.broadcasted_iota(I32, shape, dim)


def params(mib):
    return pltpu.CompilerParams(vmem_limit_bytes=int(mib * (1 << 20)))


def copies(sems, *pairs):
    found = [pltpu.make_async_copy(src, dst, sems.at[i]) for i, (src, dst) in enumerate(pairs)]
    for copy in found:
        copy.start()
    return found


def owner_rank(own_ref, step):
    sub, lane = iota((OBS, OBS), 0), iota((OBS, OBS), 1)
    across = jnp.broadcast_to(own_ref[step], (OBS, OBS)).astype(F32)
    down = jnp.sum(jnp.where(sub == lane, across, 0.0), axis=1, keepdims=True)
    same = down == across
    rank_across = jnp.sum(jnp.where(same & (sub < lane), 1.0, 0.0), axis=0, keepdims=True)
    rank_down = jnp.sum(jnp.where(same & (lane < sub), 1.0, 0.0), axis=1, keepdims=True)
    return down, across[:1], rank_down, rank_across


def request_body(own_hbm, col_hbm, out_ref, choice_ref, own_ref, col_ref, sems):
    for copy in copies(sems, (own_hbm, own_ref), (col_hbm, col_ref)):
        copy.wait()
    dest = iota((PARTS, OBS), 0).astype(F32)
    lane = iota((PARTS, BLK), 1)
    line = iota((PARTS, BLK), 0)
    from_lane = iota((OBS, PARTS * SLOTS), 1).astype(F32)
    asked = jnp.zeros((PARTS, BLK), F32)
    sends = [[], [], []]
    picks = []
    for step in range(STEPS):
        down, across, rank_down, rank_across = owner_rank(own_ref, step)
        block = col_ref[pl.ds(step, 1), :]
        group = (block * 1457) >> 16
        row = ((group & 1) * HALF + block - HALF * group) * LEV + (group >> 1)
        value = (row + 1).astype(F32)
        for nth in range(2):
            hit = (across == dest) & (rank_across == float(nth))
            found = jnp.sum(jnp.where(hit, value, 0.0), axis=1, keepdims=True)
            asked = jnp.where(lane == 2 * step + nth, found, asked)
        picks.append(jnp.where(from_lane == down * SLOTS + (2.0 * step) + rank_down, 1.0, 0.0))
        for side, shift in enumerate((0.0, 1.0, -1.0)):
            sends[side].append((across + shift) * SENT + (side * SLOTS + 2.0 * step) + rank_across)
    below = jnp.where(line == 0, 0.0, pltpu.roll(asked, 1, 0))
    above = jnp.where(line == PARTS - 1, 0.0, pltpu.roll(asked, PARTS - 1, 0))
    asked = asked + pltpu.roll(below, SLOTS, 1) + pltpu.roll(above, 2 * SLOTS, 1)
    out_ref[...] = asked.astype(I32) - 1
    pick = jnp.concatenate(picks, axis=0).astype(BF16)
    for half in range(2):
        choice_ref[pl.ds(PARTS * SENT + half * ALL_OBS, ALL_OBS), :] = pick[:, half * BLK : (half + 1) * BLK]
    spare = jnp.full((1, BLK - ALL_OBS), -1.0, F32)
    sends = [jnp.concatenate(parts + [spare], axis=1) for parts in sends]
    slot = iota((SLOTS, BLK), 0).astype(F32)
    for part in range(0, PARTS, 2):
        tiles = []
        for at in (part, part + 1):
            for side in range(3):
                tiles.append(jnp.where(sends[side] == slot + float(at * SENT + side * SLOTS), 1.0, 0.0))
        choice_ref[pl.ds(part * SENT, 2 * SENT), :] = jnp.concatenate(tiles, axis=0).astype(BF16)


def spread(tmp_ref, field):
    for run in range(LON // BLK):
        tmp_ref[run] = field[:, run * BLK : (run + 1) * BLK]
    tail = LON % BLK
    tmp_ref[LON // BLK] = jnp.concatenate(
        [field[:, LON - tail :], field[:, :PAD], field[:, LON - PAD :]], axis=1
    )


def spread_row(tmp_ref, row):
    return jnp.concatenate(
        [tmp_ref[run, pl.ds(row, LEV, stride=ROWS), :] for run in range(WIDE // BLK)], axis=1
    )


def put_row(tmp_ref, row, value):
    for run in range(WIDE // BLK):
        tmp_ref[run, pl.ds(row, LEV, stride=ROWS), :] = value[:, run * BLK : (run + 1) * BLK]


def gathered(tmp_ref):
    return jnp.concatenate([tmp_ref[run] for run in range(WIDE // BLK)], axis=1)[:, :LON]


def edges_body(inc_hbm, wts_hbm, val_hbm, wt_hbm, _, low_ref, high_ref, aux_ref, tmp_ref, inc_ref, wts_ref, sems):
    for copy in copies(
        sems,
        (inc_hbm, inc_ref),
        (wts_hbm, wts_ref),
        (val_hbm, aux_ref.at[pl.ds(0, ALL_OBS)]),
        (wt_hbm, aux_ref.at[pl.ds(ALL_OBS, ALL_OBS)]),
    ):
        copy.wait()
    spread(tmp_ref, inc_ref[...])
    for out_ref, first in ((low_ref, 0), (high_ref, HALO)):
        for row in range(0, HALO, 2):
            pair = [spread_row(tmp_ref, first + row + i)[:, :LON] for i in range(2)]
            out_ref[pl.ds(row * LEV, 2 * LEV), :] = jnp.concatenate(pair, axis=0).astype(BF16)
        rows = [wts_ref[side, first : first + HALO, :] for side in range(4)]
        out_ref[pl.ds(HALO * LEV, 4 * HALO), :] = jnp.concatenate(rows, axis=0).astype(BF16)


def widen(value):
    tail = LON % BLK
    return jnp.concatenate(
        [value[:, : LON - tail], jnp.concatenate([value[:, LON - tail :], value[:, :PAD], value[:, LON - PAD :]], axis=1)],
        axis=1,
    )


def row_of(ref, which, row):
    return jnp.broadcast_to(ref[which, pl.ds(row, 1), :], (LEV, WIDE))


def forward_body(
    inc_hbm, wts_hbm, south_ref, north_ref, table_ref, last_ref, coef_ref,
    x_ref, flat_ref, south_f, north_f, tmp_ref, inc_ref, wts_ref, sems,
):
    waits = copies(sems, (inc_hbm, inc_ref), (wts_hbm, wts_ref))
    south_f[...] = south_ref[...].astype(F32)
    north_f[...] = north_ref[...].astype(F32)
    for row in range(HALO):
        x_ref[row] = widen(south_f[pl.ds(row * LEV, LEV), :])
        x_ref[HALO + ROWS + row] = widen(north_f[pl.ds(row * LEV, LEV), :])
    for copy in waits:
        copy.wait()
    for side in range(4):
        base = HALO * LEV + side * HALO
        coef_ref[side + 1] = widen(
            jnp.concatenate([south_f[base : base + HALO, :], wts_ref[side], north_f[base : base + HALO, :]], axis=0)
        )
    coef_ref[0] = 1.0 - (coef_ref[1] + coef_ref[2] + coef_ref[3] + coef_ref[4])
    spread(tmp_ref, inc_ref[...])
    for row in range(ROWS):
        x_ref[HALO + row] = spread_row(tmp_ref, row)

    for step in range(STEPS):
        old, new = (step % 2) * EXT, ((step + 1) % 2) * EXT
        for row in range(step + 1, EXT - step - 1):
            v = x_ref[old + row]
            moved = (
                row_of(coef_ref, 0, row) * v
                + row_of(coef_ref, 1, row) * pltpu.roll(v, WIDE - 1, 1)
                + row_of(coef_ref, 2, row) * pltpu.roll(v, 1, 1)
                + row_of(coef_ref, 3, row) * x_ref[old + row + 1]
                + row_of(coef_ref, 4, row) * x_ref[old + row - 1]
            )
            x_ref[new + row] = moved
            own = row - HALO
            if 0 <= own < ROWS:
                part = own % 4
                flat_ref[own // 4, :, part * LON : (part + 1) * LON] = moved[:, :LON]
        for pair in range(HALF):
            tiles = []
            for tile in (2 * pair, 2 * pair + 1):
                half, at = tile // HALF, tile % HALF
                tiles.append(flat_ref[half, :, at * BLK : (at + 1) * BLK])
            table_ref[step, pl.ds(pair * 2 * LEV, 2 * LEV), :] = jnp.concatenate(tiles, axis=0).astype(BF16)
    final = (STEPS % 2) * EXT + HALO
    for row in range(ROWS):
        put_row(tmp_ref, row, x_ref[final + row])
    last_ref[...] = gathered(tmp_ref).astype(BF16)


def gather_body(asked_ref, table_ref, _, out_ref, __, slots_ref):
    lane = iota((PARTS, BLOCKS), 1)
    asked = asked_ref[...]
    for step in range(STEPS):
        picks = [
            jnp.where(asked[:, 2 * step + nth : 2 * step + nth + 1] == lane, 1.0, 0.0).astype(BF16)
            for nth in range(2)
        ]
        blocks = jnp.dot(jnp.concatenate(picks, axis=0), table_ref[step], preferred_element_type=F32)
        for nth in range(2):
            slots_ref[pl.ds(2 * step + nth, PARTS, stride=SLOTS), :] = blocks[nth * PARTS : (nth + 1) * PARTS]
    out_ref[...] = slots_ref[...].astype(BF16)


def misfit_body(
    first_ref, inc_hbm, weight_hbm, back_hbm, prev_ref, out_ref, own_ref, low_ref, high_ref, token_ref,
    tmp_ref, inc_ref, weight_ref, back_ref, sems,
):
    for copy in copies(sems, (inc_hbm, inc_ref), (weight_hbm, weight_ref), (back_hbm, back_ref)):
        copy.wait()
    begin = jnp.where(first_ref[0] == 1, back_ref[...], prev_ref[...].astype(F32))
    misfit = weight_ref[...] * (inc_ref[...] - begin)
    out_ref[...] = misfit
    token_ref[...] = misfit[:8, :BLK]
    spread(tmp_ref, misfit)
    for row in range(0, ROWS, 2):
        pair = [spread_row(tmp_ref, row + i)[:, :LON] for i in range(2)]
        both = jnp.concatenate(pair, axis=0).astype(BF16)
        own_ref[pl.ds(row * LEV, 2 * LEV), :] = both
        if row < HALO:
            low_ref[pl.ds(row * LEV, 2 * LEV), :] = both
        else:
            high_ref[pl.ds((row - HALO) * LEV, 2 * LEV), :] = both


def spread_out(block):
    line = iota(block.shape, 0)
    zero = jnp.zeros_like(block)
    return jnp.concatenate([jnp.where(line == i, block, zero) for i in range(block.shape[0])], axis=1)


GROUP = 16


def observe_body(
    got_ref, choice_hbm, aux_hbm, ops_hbm, _, dep_ref, out_ref, choice_ref, aux_ref, ops_ref, sems
):
    size = GROUP * BLK
    parts = [pl.ds(first, size) for first in range(0, ALL_OBS * BLK, size)]
    pairs = [(choice_hbm, choice_ref), (aux_hbm, aux_ref)]
    waits = copies(sems, *pairs, *[(ops_hbm.at[part], ops_ref.at[part]) for part in parts])
    waits[0].wait()
    base = PARTS * SENT
    pick = jnp.concatenate([choice_ref[base + half * ALL_OBS : base + (half + 1) * ALL_OBS, :] for half in range(2)], axis=1)
    seen = jnp.dot(pick, got_ref[...], preferred_element_type=F32).astype(BF16)
    waits[1].wait()
    line = iota((GROUP, BLK), 0)
    scaled = []
    for at in range(ALL_OBS // GROUP):
        waits[2 + at].wait()
        first = at * GROUP
        rows = slice(first, first + GROUP)
        product = jnp.zeros((GROUP, BLK), F32)
        for i in range(GROUP):
            one = lax.dot_general(
                seen[rows],
                ops_ref[(first + i) * BLK : (first + i + 1) * BLK, :],
                (((1,), (1,)), ((), ())),
                preferred_element_type=F32,
            )
            product = jnp.where(line == i, one, product)
        departure = product - aux_ref[first : first + GROUP, :]
        dep_ref[rows, :] = departure
        weight = aux_ref[ALL_OBS + first : ALL_OBS + first + GROUP, :]
        scaled.append((weight * departure).astype(BF16))
    steps = []
    for at, block in enumerate(scaled):
        first = at * GROUP
        steps.append(
            jnp.dot(
                spread_out(block), ops_ref[first * BLK : (first + GROUP) * BLK, :], preferred_element_type=F32
            ).astype(BF16)
        )
    increments = jnp.concatenate(steps, axis=0)
    out_ref[...] = jnp.dot(choice_ref[:base, :ALL_OBS], increments, preferred_element_type=F32).astype(BF16)


PAIRS = ((2, 3), (0, 1))
SIDES = ((0, 0, 0, BLOCKS), (1, BLOCKS, HALF * LEV, HALF * LEV), (2, BLOCKS + HALF * LEV, 0, HALF * LEV))


def prepare_body(asked_ref, lam_ref, south_ref, north_ref, dep_ref, put_ref, y_ref, out_ref):
    out_ref[...] = dep_ref[...]
    asked = jnp.transpose(asked_ref[...].astype(F32))
    for at, steps in enumerate(PAIRS):
        for side, base, start, size in SIDES:
            named = jnp.concatenate(
                [asked[side * SLOTS + 2 * step + nth :][:1] for step in steps for nth in range(2)], axis=1
            )
            line = (iota((size, 4 * PARTS), 0) + start).astype(F32)
            put_ref[at, base : base + size, :] = jnp.where(line == named, 1.0, 0.0).astype(BF16)
    for block_ref, first, rows in ((south_ref, 0, HALO), (lam_ref, HALO, ROWS), (north_ref, HALO + ROWS, HALO)):
        for row in range(0, rows, 2):
            both = block_ref[pl.ds(row * LEV, 2 * LEV), :].astype(F32)
            for i in range(2):
                y_ref[first + row + i] = -widen(both[i * LEV : (i + 1) * LEV])


def adjoint_body(got_ref, put_ref, first_ref, misfit_ref, coef_ref, out_ref, got_f, flat_ref, a_ref, y_ref, tmp_ref):
    got_f[...] = got_ref[...].astype(F32)
    for at, steps in enumerate(PAIRS):
        for side, base, start, size in SIDES:
            sides = []
            for i, step in enumerate(steps):
                terms = jnp.concatenate(
                    [got_f[pl.ds(side * SLOTS + 2 * step + nth, PARTS, stride=SENT), :] for nth in range(2)], axis=0
                ).astype(BF16)
                zero = jnp.zeros_like(terms)
                sides.append(jnp.concatenate([terms, zero] if i == 0 else [zero, terms], axis=0))
            added = jnp.dot(
                put_ref[at, base : base + size, :], jnp.concatenate(sides, axis=1), preferred_element_type=F32
            )
            flat = (1, 0, 3)[side]
            for i, step in enumerate(steps):
                for tile in range(size // LEV):
                    half, run = tile // HALF, tile % HALF
                    flat_ref[step * 4 + flat + half, :, run * BLK : (run + 1) * BLK] = added[
                        tile * LEV : (tile + 1) * LEV, i * BLK : (i + 1) * BLK
                    ]
    for step in range(STEPS - 1, -1, -1):
        edge = STEPS - 1 - step
        before = first_ref if edge == 0 else y_ref
        for row in range(edge, EXT - edge):
            part = row % 4
            a_ref[row] = before[row] + widen(flat_ref[step * 4 + row // 4, :, part * LON : (part + 1) * LON])
        for row in range(edge + 1, EXT - edge - 1):
            v = a_ref[row]
            pulled = (
                row_of(coef_ref, 0, row) * v
                + pltpu.roll(row_of(coef_ref, 1, row) * v, 1, 1)
                + pltpu.roll(row_of(coef_ref, 2, row) * v, WIDE - 1, 1)
                + row_of(coef_ref, 3, row - 1) * a_ref[row - 1]
                + row_of(coef_ref, 4, row + 1) * a_ref[row + 1]
            )
            if step:
                y_ref[row] = pulled
            else:
                put_row(tmp_ref, row - HALO, pulled)
    out_ref[...] = gathered(tmp_ref) + misfit_ref[...]


def shape(dims, dtype):
    return jax.ShapeDtypeStruct(dims, dtype)


def exchange(block):
    return lax.all_to_all(block, "space", split_axis=0, concat_axis=0, tiled=True)


def local(
    increments,
    background,
    error_weight,
    neighbor_weights,
    operators,
    values,
    obs_weight,
    owners,
    columns,
):
    fields = LEV * ROWS
    start = increments.reshape(fields, LON)
    owner = owners.reshape(STEPS, 1, OBS)
    windows, parts = lax.axis_size("tm"), lax.axis_size("space")
    vmem = pl.BlockSpec(memory_space=pltpu.VMEM)
    home = pl.BlockSpec(memory_space=pltpu.HBM)
    anywhere = pl.BlockSpec(memory_space=pl.ANY)
    sems = pltpu.SemaphoreType.DMA
    field = pltpu.VMEM((fields, LON), F32)
    weights = pltpu.VMEM((4, ROWS, LON), F32)
    runs = pltpu.VMEM((WIDE // BLK, fields, BLK), F32)
    wide = pltpu.VMEM((EXT, LEV, WIDE), F32)

    request, choice = pl.pallas_call(
        request_body,
        in_specs=[home, home],
        out_shape=(
            shape((PARTS, BLK), I32),
            shape((PARTS * SENT + 2 * ALL_OBS, BLK), BF16),
        ),
        scratch_shapes=[pltpu.VMEM((STEPS, 1, OBS), I32), pltpu.VMEM((STEPS, OBS), I32), sems((2,))],
        name="request",
        compiler_params=params(60),
    )(owner, columns.reshape(STEPS, OBS))
    asked = exchange(request)

    edge = shape((HALO * LEV + 4 * HALO, LON), BF16)
    low, high, aux = pl.pallas_call(
        edges_body,
        in_specs=[home, home, home, home, anywhere],
        out_shape=(edge, edge, shape((2 * ALL_OBS, BLK), F32)),
        scratch_shapes=[runs, field, weights, sems((4,))],
        name="edges",
        compiler_params=params(60),
    )(start, neighbor_weights, values.reshape(ALL_OBS, BLK), obs_weight.reshape(ALL_OBS, BLK), request)
    south = lax.ppermute(high, "space", [(i, i + 1) for i in range(parts - 1)])
    north = lax.ppermute(low, "space", [(i + 1, i) for i in range(parts - 1)])

    edge_f = pltpu.VMEM((HALO * LEV + 4 * HALO, LON), F32)
    tables, last, coeffs = pl.pallas_call(
        forward_body,
        in_specs=[home, home, vmem, vmem],
        out_shape=(
            shape((STEPS, BLOCKS, BLK), BF16),
            shape((fields, LON), BF16),
            shape((5, EXT, WIDE), F32),
        ),
        scratch_shapes=[
            pltpu.VMEM((2 * EXT, LEV, WIDE), F32),
            pltpu.VMEM((2, LEV, HALF * BLK), F32),
            edge_f,
            edge_f,
            runs,
            field,
            weights,
            sems((2,)),
        ],
        name="forward",
        compiler_params=params(20),
    )(start, neighbor_weights, south, north)

    blocks, last = pl.pallas_call(
        gather_body,
        in_specs=[vmem, vmem, anywhere],
        out_specs=(vmem, anywhere),
        out_shape=(shape((PARTS * SLOTS, BLK), BF16), shape((fields, LON), BF16)),
        input_output_aliases={2: 1},
        scratch_shapes=[pltpu.VMEM((PARTS * SLOTS, BLK), F32)],
        name="gather",
        compiler_params=params(16),
    )(asked, tables, last)
    got = exchange(blocks)

    previous = lax.ppermute(last, "tm", [(i, i + 1) for i in range(windows - 1)])
    first = (lax.axis_index("tm") == 0).astype(I32).reshape(1)
    side = shape((HALO * LEV, LON), BF16)
    misfit, sent, sent_low, sent_high, token = pl.pallas_call(
        misfit_body,
        in_specs=[pl.BlockSpec(memory_space=pltpu.SMEM), home, home, home, vmem],
        out_shape=(shape((fields, LON), F32), shape((fields, LON), BF16), side, side, shape((8, BLK), F32)),
        scratch_shapes=[runs, field, field, field, sems((3,))],
        name="misfit",
        compiler_params=params(16),
    )(first, start, error_weight.reshape(fields, LON), background.reshape(fields, LON), previous)

    def back(block, shift):
        route = []
        for k in range(1, windows):
            for p in range(parts):
                if 0 <= p + shift < parts:
                    route.append((k * parts + p, (k - 1) * parts + p + shift))
        return lax.ppermute(block, ("tm", "space"), route)

    lam = back(sent, 0)
    lam_south = back(sent_high, 1)
    lam_north = back(sent_low, -1)

    per_obs = shape((ALL_OBS, BLK), F32)
    found, slots = pl.pallas_call(
        observe_body,
        in_specs=[vmem] + [home] * 3 + [anywhere],
        out_shape=(per_obs, shape((PARTS * SENT, BLK), BF16)),
        scratch_shapes=[
            pltpu.VMEM((PARTS * SENT + 2 * ALL_OBS, BLK), BF16),
            pltpu.VMEM((2 * ALL_OBS, BLK), F32),
            pltpu.VMEM((ALL_OBS * BLK, BLK), BF16),
            sems((2 + ALL_OBS // GROUP,)),
        ],
        name="observe",
        compiler_params=params(53.75),
    )(
        got,
        choice,
        aux,
        operators.reshape(ALL_OBS * BLK, BLK),
        token,
    )
    arrived = exchange(slots)

    put, ahead, departures = pl.pallas_call(
        prepare_body,
        out_shape=(shape((2, 2 * BLOCKS, BLK), BF16), shape((EXT, LEV, WIDE), F32), per_obs),
        name="prepare",
        compiler_params=params(16),
    )(asked, lam, lam_south, lam_north, found)

    gradient = pl.pallas_call(
        adjoint_body,
        out_shape=shape((fields, LON), F32),
        scratch_shapes=[
            pltpu.VMEM((PARTS * SENT, BLK), F32),
            pltpu.VMEM((4 * STEPS, LEV, HALF * BLK), F32),
            wide,
            wide,
            runs,
        ],
        name="adjoint",
        compiler_params=params(20),
    )(arrived, put, ahead, misfit, coeffs)
    return (gradient.reshape(increments.shape), departures.reshape(values.shape))


def solution(mesh):
    in_specs = (
        P("tm", None, "space", None),
        P(None, "space", None),
        P(None, "space", None),
        P(None, "space", None),
        P("tm", None, "space", None, None),
        P("tm", None, "space", None),
        P("tm", None, "space", None),
        P("tm", None, "space", None),
        P("tm", None, "space"),
    )
    out_specs = (P("tm", None, "space", None), P("tm", None, "space", None))
    return jax.shard_map(local, mesh=mesh, in_specs=in_specs, out_specs=out_specs, check_vma=False)
```

```python
import jax
import jax.numpy as jnp
from jax import lax
from jax.experimental import pallas as pl
from jax.experimental.pallas import tpu as pltpu
from jax.sharding import PartitionSpec as P

LEV = 8
ROWS = 8
LON = 1440
WIDE = 1536
PAD = 48
STEPS = 4
HALO = 4
EXT = ROWS + 2 * HALO
FULL = 3 * ROWS
FIELD = LEV * ROWS
SENT_ROWS = FIELD + 4 * ROWS + FIELD
OBS = 24
ALL_OBS = STEPS * OBS
BLK = 128
PARTS = 32
SLOTS = 2 * STEPS
SENT = 3 * SLOTS
HALF = 45
BLOCKS = 2 * HALF * LEV
F32 = jnp.float32
BF16 = jnp.bfloat16
I32 = jnp.int32


def iota(shape, dim):
    return lax.broadcasted_iota(I32, shape, dim)


def params(mib):
    return pltpu.CompilerParams(vmem_limit_bytes=int(mib * (1 << 20)))


def copies(sems, *pairs):
    found = [pltpu.make_async_copy(src, dst, sems.at[i]) for i, (src, dst) in enumerate(pairs)]
    for copy in found:
        copy.start()
    return found


def owner_rank(own_ref, step):
    sub, lane = iota((OBS, OBS), 0), iota((OBS, OBS), 1)
    across = jnp.broadcast_to(own_ref[step], (OBS, OBS)).astype(F32)
    down = jnp.sum(jnp.where(sub == lane, across, 0.0), axis=1, keepdims=True)
    same = down == across
    rank_across = jnp.sum(jnp.where(same & (sub < lane), 1.0, 0.0), axis=0, keepdims=True)
    rank_down = jnp.sum(jnp.where(same & (lane < sub), 1.0, 0.0), axis=1, keepdims=True)
    return down, across[:1], rank_down, rank_across


def request_body(own_hbm, col_hbm, _, out_ref, choice_ref, own_ref, col_ref, sems):
    for copy in copies(sems, (own_hbm, own_ref), (col_hbm, col_ref)):
        copy.wait()
    dest = iota((PARTS, OBS), 0).astype(F32)
    lane = iota((PARTS, BLK), 1)
    line = iota((PARTS, BLK), 0)
    from_lane = iota((OBS, PARTS * SLOTS), 1).astype(F32)
    asked = jnp.zeros((PARTS, BLK), F32)
    sends = [[], [], []]
    picks = []
    for step in range(STEPS):
        down, across, rank_down, rank_across = owner_rank(own_ref, step)
        block = col_ref[pl.ds(step, 1), :]
        group = (block * 1457) >> 16
        row = ((group & 1) * HALF + block - HALF * group) * LEV + (group >> 1)
        value = (row + 1).astype(F32)
        for nth in range(2):
            hit = (across == dest) & (rank_across == float(nth))
            found = jnp.sum(jnp.where(hit, value, 0.0), axis=1, keepdims=True)
            asked = jnp.where(lane == 2 * step + nth, found, asked)
        picks.append(jnp.where(from_lane == down * SLOTS + (2.0 * step) + rank_down, 1.0, 0.0))
        for side, shift in enumerate((0.0, 1.0, -1.0)):
            sends[side].append((across + shift) * SENT + (side * SLOTS + 2.0 * step) + rank_across)
    below = jnp.where(line == 0, 0.0, pltpu.roll(asked, 1, 0))
    above = jnp.where(line == PARTS - 1, 0.0, pltpu.roll(asked, PARTS - 1, 0))
    asked = asked + pltpu.roll(below, SLOTS, 1) + pltpu.roll(above, 2 * SLOTS, 1)
    out_ref[...] = asked.astype(I32) - 1
    pick = jnp.concatenate(picks, axis=0).astype(BF16)
    for half in range(2):
        choice_ref[pl.ds(PARTS * SENT + half * ALL_OBS, ALL_OBS), :] = pick[:, half * BLK : (half + 1) * BLK]
    spare = jnp.full((1, BLK - ALL_OBS), -1.0, F32)
    sends = [jnp.concatenate(parts + [spare], axis=1) for parts in sends]
    slot = iota((SLOTS, BLK), 0).astype(F32)
    for part in range(0, PARTS, 2):
        tiles = []
        for at in (part, part + 1):
            for side in range(3):
                tiles.append(jnp.where(sends[side] == slot + float(at * SENT + side * SLOTS), 1.0, 0.0))
        choice_ref[pl.ds(part * SENT, 2 * SENT), :] = jnp.concatenate(tiles, axis=0).astype(BF16)


def spread(tmp_ref, field):
    for run in range(LON // BLK):
        tmp_ref[run] = field[:, run * BLK : (run + 1) * BLK]
    tail = LON % BLK
    tmp_ref[LON // BLK] = jnp.concatenate(
        [field[:, LON - tail :], field[:, :PAD], field[:, LON - PAD :]], axis=1
    )


def spread_row(tmp_ref, row):
    return jnp.concatenate(
        [tmp_ref[run, pl.ds(row, LEV, stride=ROWS), :] for run in range(WIDE // BLK)], axis=1
    )


def put_row(tmp_ref, row, value):
    for run in range(WIDE // BLK):
        tmp_ref[run, pl.ds(row, LEV, stride=ROWS), :] = value[:, run * BLK : (run + 1) * BLK]


def gathered(tmp_ref):
    return jnp.concatenate([tmp_ref[run] for run in range(WIDE // BLK)], axis=1)[:, :LON]


def edges_body(inc_hbm, wts_hbm, err_hbm, val_hbm, wt_hbm, out_ref, own_ref, aux_ref, err_ref, sems):
    for copy in copies(
        sems,
        (inc_hbm, own_ref.at[pl.ds(0, FIELD)]),
        (wts_hbm, own_ref.at[pl.ds(FIELD, 4 * ROWS)]),
        (err_hbm, err_ref),
        (val_hbm, aux_ref.at[pl.ds(0, ALL_OBS)]),
        (wt_hbm, aux_ref.at[pl.ds(ALL_OBS, ALL_OBS)]),
    ):
        copy.wait()
    out_ref[0 : FIELD + 4 * ROWS, :] = own_ref[...].astype(BF16)
    out_ref[FIELD + 4 * ROWS : SENT_ROWS, :] = err_ref[...].astype(BF16)


def widen(value):
    tail = LON % BLK
    return jnp.concatenate(
        [value[:, : LON - tail], jnp.concatenate([value[:, LON - tail :], value[:, :PAD], value[:, LON - PAD :]], axis=1)],
        axis=1,
    )


def row_of(ref, which, row):
    return jnp.broadcast_to(ref[which, pl.ds(row, 1), :], (LEV, WIDE))


def forward_body(
    own_hbm, south_ref, north_ref, t1_ref, t2_ref, t3_ref, t4_ref, last_ref, next_ref, pack_ref,
    x_ref, flat_ref, wide_ref, low_tmp, own_tmp, high_tmp, own_ref, sems,
):
    (wait,) = copies(sems, (own_hbm, own_ref))
    spread(low_tmp, south_ref[FIELD + 4 * ROWS :, :].astype(F32))
    spread(high_tmp, north_ref[FIELD + 4 * ROWS :, :].astype(F32))
    for row in range(HALO):
        pack_ref[EXT + row] = spread_row(low_tmp, HALO + row)
        pack_ref[EXT + HALO + row] = spread_row(high_tmp, row)
    spread(low_tmp, south_ref[0:FIELD, :].astype(F32))
    spread(high_tmp, north_ref[0:FIELD, :].astype(F32))
    for row in range(ROWS):
        x_ref[row] = spread_row(low_tmp, row)
        x_ref[2 * ROWS + row] = spread_row(high_tmp, row)
    wait.wait()
    spread(own_tmp, own_ref[0:FIELD, :])
    for row in range(ROWS):
        x_ref[ROWS + row] = spread_row(own_tmp, row)
    for side in range(4):
        rows = slice(FIELD + side * ROWS, FIELD + (side + 1) * ROWS)
        for i, part_ref in enumerate((south_ref, own_ref, north_ref)):
            wide_ref[side + 1, i * ROWS : (i + 1) * ROWS, :] = widen(part_ref[rows, :].astype(F32))
    wide_ref[0] = 1.0 - (wide_ref[1] + wide_ref[2] + wide_ref[3] + wide_ref[4])
    for side in range(5):
        for half in range(2):
            first = HALO + half * ROWS
            pack_ref[EXT + ROWS + 2 * side + half] = wide_ref[side, first : first + ROWS, :]
    for row in range(0, EXT, 2):
        pair = [x_ref[HALO + row + i][:, :LON] for i in range(2)]
        next_ref[pl.ds(row * LEV, 2 * LEV), :] = jnp.concatenate(pair, axis=0).astype(BF16)

    for step in range(STEPS):
        old, new = (step % 2) * FULL, ((step + 1) % 2) * FULL
        for row in range(step + 1, FULL - step - 1):
            v = x_ref[old + row]
            moved = (
                row_of(wide_ref, 0, row) * v
                + row_of(wide_ref, 1, row) * pltpu.roll(v, WIDE - 1, 1)
                + row_of(wide_ref, 2, row) * pltpu.roll(v, 1, 1)
                + row_of(wide_ref, 3, row) * x_ref[old + row + 1]
                + row_of(wide_ref, 4, row) * x_ref[old + row - 1]
            )
            own = row - ROWS
            if step < STEPS - 1:
                x_ref[new + row] = moved
            else:
                pack_ref[row - HALO] = moved
                if 0 <= own < ROWS:
                    put_row(own_tmp, own, moved)
            if 0 <= own < ROWS:
                part = own % 4
                flat_ref[own // 4, :, part * LON : (part + 1) * LON] = moved[:, :LON]
        for pair in range(HALF):
            tiles = []
            for tile in (2 * pair, 2 * pair + 1):
                half, at = tile // HALF, tile % HALF
                tiles.append(flat_ref[half, :, at * BLK : (at + 1) * BLK])
            (t1_ref, t2_ref, t3_ref, t4_ref)[step][pl.ds(pair * 2 * LEV, 2 * LEV), :] = jnp.concatenate(tiles, axis=0).astype(BF16)
    last_ref[...] = gathered(own_tmp).astype(BF16)


def gather_body(asked_ref, t1_ref, t2_ref, t3_ref, t4_ref, out_ref, token_ref, slots_ref):
    lane = iota((PARTS, BLOCKS), 1)
    asked = asked_ref[...]
    for step in range(STEPS):
        picks = [
            jnp.where(asked[:, 2 * step + nth : 2 * step + nth + 1] == lane, 1.0, 0.0).astype(BF16)
            for nth in range(2)
        ]
        blocks = jnp.dot(jnp.concatenate(picks, axis=0), (t1_ref, t2_ref, t3_ref, t4_ref)[step][...], preferred_element_type=F32)
        for nth in range(2):
            slots_ref[pl.ds(2 * step + nth, PARTS, stride=SLOTS), :] = blocks[nth * PARTS : (nth + 1) * PARTS]
    out_ref[...] = slots_ref[...].astype(BF16)
    token_ref[...] = slots_ref[0:8, :]


def hold_body(token_ref, last_in, next_in, last_out, next_out, seen_ref):
    seen_ref[...] = token_ref[...]


def spread_out(block):
    line = iota(block.shape, 0)
    zero = jnp.zeros_like(block)
    return jnp.concatenate([jnp.where(line == i, block, zero) for i in range(block.shape[0])], axis=1)


GROUP = 16


def observe_body(
    got_ref, choice_hbm, aux_hbm, ops_hbm, _, dep_ref, out_ref, choice_ref, aux_ref, ops_ref, sems
):
    size = GROUP * BLK
    parts = [pl.ds(first, size) for first in range(0, ALL_OBS * BLK, size)]
    pairs = [(choice_hbm, choice_ref), (aux_hbm, aux_ref)]
    waits = copies(sems, *pairs, *[(ops_hbm.at[part], ops_ref.at[part]) for part in parts])
    waits[0].wait()
    base = PARTS * SENT
    pick = jnp.concatenate([choice_ref[base + half * ALL_OBS : base + (half + 1) * ALL_OBS, :] for half in range(2)], axis=1)
    seen = jnp.dot(pick, got_ref[...], preferred_element_type=F32).astype(BF16)
    waits[1].wait()
    line = iota((GROUP, BLK), 0)
    scaled = []
    for at in range(ALL_OBS // GROUP):
        waits[2 + at].wait()
        first = at * GROUP
        rows = slice(first, first + GROUP)
        product = jnp.zeros((GROUP, BLK), F32)
        for i in range(0, GROUP, 2):
            two = lax.dot_general(
                seen[rows],
                ops_ref[(first + i) * BLK : (first + i + 2) * BLK, :],
                (((1,), (1,)), ((), ())),
                preferred_element_type=F32,
            )
            product = jnp.where(line == i, two[:, :BLK], product)
            product = jnp.where(line == i + 1, two[:, BLK:], product)
        departure = product - aux_ref[first : first + GROUP, :]
        dep_ref[rows, :] = departure
        weight = aux_ref[ALL_OBS + first : ALL_OBS + first + GROUP, :]
        scaled.append((weight * departure).astype(BF16))
    steps = []
    for at, block in enumerate(scaled):
        first = at * GROUP
        steps.append(
            jnp.dot(
                spread_out(block), ops_ref[first * BLK : (first + GROUP) * BLK, :], preferred_element_type=F32
            ).astype(BF16)
        )
    increments = jnp.concatenate(steps, axis=0)
    out_ref[...] = jnp.dot(choice_ref[:base, :ALL_OBS], increments, preferred_element_type=F32).astype(BF16)


PAIRS = ((2, 3), (0, 1))
SIDES = ((0, 0, 0, BLOCKS), (1, BLOCKS, HALF * LEV, HALF * LEV), (2, BLOCKS + HALF * LEV, 0, HALF * LEV))


def put_body(asked_ref, late_ref, early_ref):
    asked = jnp.transpose(asked_ref[...].astype(F32))
    for at, steps in enumerate(PAIRS):
        for side, base, start, size in SIDES:
            named = jnp.concatenate(
                [asked[side * SLOTS + 2 * step + nth :][:1] for step in steps for nth in range(2)], axis=1
            )
            line = (iota((size, 4 * PARTS), 0) + start).astype(F32)
            (late_ref, early_ref)[at][base : base + size, :] = jnp.where(line == named, 1.0, 0.0).astype(BF16)


def prepare_body(
    next_ref, err_ref, dep_ref, pack_hbm, a_ref, b_ref, c_ref, d_ref, out_ref, *rest
):
    *coef_refs, own_tmp, pack_ref, sems = rest
    (wait,) = copies(sems, (pack_hbm, pack_ref))
    out_ref[...] = dep_ref[...]
    spread(own_tmp, err_ref[...])
    wait.wait()
    final = lax.axis_index("tm") == lax.axis_size("tm") - 1
    for row in range(0, EXT, 2):
        both = next_ref[pl.ds(row * LEV, 2 * LEV), :].astype(F32)
        for i in range(2):
            at = row + i - HALO
            if 0 <= at < ROWS:
                weight = spread_row(own_tmp, at)
            else:
                weight = pack_ref[EXT + (row + i) % ROWS]
            ahead = weight * (pack_ref[row + i] - widen(both[i * LEV : (i + 1) * LEV]))
            (a_ref, b_ref, c_ref, d_ref)[row // 4][(row + i) % 4] = jnp.where(final, 0.0, ahead)
    for which, coef_ref in enumerate(coef_refs):
        for half in range(2):
            coef_ref[half * ROWS : (half + 1) * ROWS, :] = pack_ref[EXT + ROWS + 2 * which + half]


def adjoint_body(got_ref, prev_ref, late_ref, early_ref, *rest):
    first_refs, coef_refs = rest[:4], rest[4:9]
    inc_hbm, err_hbm, back_hbm, out_ref, got_f, flat_ref, a_ref, y_ref, tmp_ref, inc_ref, err_ref, back_ref, sems = rest[9:]
    waits = copies(sems, (inc_hbm, inc_ref), (err_hbm, err_ref), (back_hbm, back_ref))

    def weight(which, row):
        return jnp.broadcast_to(coef_refs[which][pl.ds(row, 1), :], (LEV, WIDE))

    got_f[...] = got_ref[...].astype(F32)
    for at, steps in enumerate(PAIRS):
        for side, base, start, size in SIDES:
            sides = []
            for i, step in enumerate(steps):
                terms = jnp.concatenate(
                    [got_f[pl.ds(side * SLOTS + 2 * step + nth, PARTS, stride=SENT), :] for nth in range(2)], axis=0
                ).astype(BF16)
                zero = jnp.zeros_like(terms)
                sides.append(jnp.concatenate([terms, zero] if i == 0 else [zero, terms], axis=0))
            added = jnp.dot(
                (late_ref, early_ref)[at][base : base + size, :],
                jnp.concatenate(sides, axis=1),
                preferred_element_type=F32
            )
            flat = (1, 0, 3)[side]
            for i, step in enumerate(steps):
                for tile in range(size // LEV):
                    half, run = tile // HALF, tile % HALF
                    flat_ref[step * 4 + flat + half, :, run * BLK : (run + 1) * BLK] = added[
                        tile * LEV : (tile + 1) * LEV, i * BLK : (i + 1) * BLK
                    ]
    for step in range(STEPS - 1, -1, -1):
        edge = STEPS - 1 - step
        for row in range(edge, EXT - edge):
            part = row % 4
            before = first_refs[row // 4][row % 4] if edge == 0 else y_ref[row]
            a_ref[row] = before + widen(flat_ref[step * 4 + row // 4, :, part * LON : (part + 1) * LON])
        for row in range(edge + 1, EXT - edge - 1):
            v = a_ref[row]
            pulled = (
                weight(0, row) * v
                + pltpu.roll(weight(1, row) * v, 1, 1)
                + pltpu.roll(weight(2, row) * v, WIDE - 1, 1)
                + weight(3, row - 1) * a_ref[row - 1]
                + weight(4, row + 1) * a_ref[row + 1]
            )
            if step:
                y_ref[row] = pulled
            else:
                put_row(tmp_ref, row - HALO, pulled)
    for wait in waits:
        wait.wait()
    begin = jnp.where(lax.axis_index("tm") == 0, back_ref[...], prev_ref[...].astype(F32))
    out_ref[...] = gathered(tmp_ref) + err_ref[...] * (inc_ref[...] - begin)


def shape(dims, dtype):
    return jax.ShapeDtypeStruct(dims, dtype)


def exchange(block):
    return lax.all_to_all(block, "space", split_axis=0, concat_axis=0, tiled=True)


def local(
    increments,
    background,
    error_weight,
    neighbor_weights,
    operators,
    values,
    obs_weight,
    owners,
    columns,
):
    fields = LEV * ROWS
    start = increments.reshape(fields, LON)
    owner = owners.reshape(STEPS, 1, OBS)
    windows, parts = lax.axis_size("tm"), lax.axis_size("space")
    vmem = pl.BlockSpec(memory_space=pltpu.VMEM)
    home = pl.BlockSpec(memory_space=pltpu.HBM)
    anywhere = pl.BlockSpec(memory_space=pl.ANY)
    sems = pltpu.SemaphoreType.DMA
    field = pltpu.VMEM((fields, LON), F32)
    runs = pltpu.VMEM((WIDE // BLK, fields, BLK), F32)
    wide = pltpu.VMEM((EXT, LEV, WIDE), F32)

    err = error_weight.reshape(fields, LON)
    stencil = neighbor_weights.reshape(4 * ROWS, LON)
    edge, own, aux = pl.pallas_call(
        edges_body,
        in_specs=[home] * 5,
        out_shape=(
            shape((SENT_ROWS, LON), BF16),
            shape((FIELD + 4 * ROWS, LON), F32),
            shape((2 * ALL_OBS, BLK), F32),
        ),
        scratch_shapes=[field, sems((5,))],
        name="edges",
        compiler_params=params(60),
    )(start, stencil, err, values.reshape(ALL_OBS, BLK), obs_weight.reshape(ALL_OBS, BLK))
    south = lax.ppermute(edge, "space", [(i, i + 1) for i in range(parts - 1)])
    north = lax.ppermute(edge, "space", [(i + 1, i) for i in range(parts - 1)])

    request, choice = pl.pallas_call(
        request_body,
        in_specs=[home, home, anywhere],
        out_shape=(
            shape((PARTS, BLK), I32),
            shape((PARTS * SENT + 2 * ALL_OBS, BLK), BF16),
        ),
        scratch_shapes=[pltpu.VMEM((STEPS, 1, OBS), I32), pltpu.VMEM((STEPS, OBS), I32), sems((2,))],
        name="request",
        compiler_params=params(60),
    )(owner, columns.reshape(STEPS, OBS), aux)
    asked = exchange(request)

    around = shape((EXT * LEV, LON), BF16)
    here = shape((fields, LON), BF16)
    *tables, last, following, pack = pl.pallas_call(
        forward_body,
        in_specs=[home, vmem, vmem],
        out_shape=(
            *[shape((BLOCKS, BLK), BF16) for _ in range(STEPS)],
            here,
            around,
            shape((EXT + ROWS + 10, LEV, WIDE), F32),
        ),
        scratch_shapes=[
            pltpu.VMEM((2 * FULL, LEV, WIDE), F32),
            pltpu.VMEM((2, LEV, HALF * BLK), F32),
            pltpu.VMEM((5, FULL, WIDE), F32),
            runs,
            runs,
            runs,
            pltpu.VMEM((FIELD + 4 * ROWS, LON), F32),
            sems((1,)),
        ],
        name="forward",
        compiler_params=params(51.45),
    )(own, south, north)

    mark = shape((8, BLK), F32)
    blocks, token = pl.pallas_call(
        gather_body,
        out_shape=(shape((PARTS * SLOTS, BLK), BF16), mark),
        scratch_shapes=[pltpu.VMEM((PARTS * SLOTS, BLK), F32)],
        name="gather",
        compiler_params=params(16),
    )(asked, *tables)
    got = exchange(blocks)

    last, following, token = pl.pallas_call(
        hold_body,
        in_specs=[vmem, anywhere, anywhere],
        out_specs=(anywhere, anywhere, vmem),
        out_shape=(here, around, mark),
        input_output_aliases={1: 0, 2: 1},
        name="hold",
        cost_estimate=pl.CostEstimate(flops=0, transcendentals=0, bytes_accessed=30_000_000),
        compiler_params=params(16),
    )(token, last, following)
    previous = lax.ppermute(last, "tm", [(i, i + 1) for i in range(windows - 1)])
    following = lax.ppermute(following, "tm", [(i + 1, i) for i in range(windows - 1)])

    per_obs = shape((ALL_OBS, BLK), F32)
    found, slots = pl.pallas_call(
        observe_body,
        in_specs=[vmem] + [home] * 3 + [anywhere],
        out_shape=(per_obs, shape((PARTS * SENT, BLK), BF16)),
        scratch_shapes=[
            pltpu.VMEM((PARTS * SENT + 2 * ALL_OBS, BLK), BF16),
            pltpu.VMEM((2 * ALL_OBS, BLK), F32),
            pltpu.VMEM((ALL_OBS * BLK, BLK), BF16),
            sems((2 + ALL_OBS // GROUP,)),
        ],
        name="observe",
        compiler_params=params(53.75),
    )(got, choice, aux, operators.reshape(ALL_OBS * BLK, BLK), following)
    arrived = exchange(slots)

    half = shape((2 * BLOCKS, BLK), BF16)
    put = pl.pallas_call(put_body, out_shape=(half, half), name="put", compiler_params=params(16))(asked)
    quarter = shape((4, LEV, WIDE), F32)
    *ahead, departures, c, e, w, n, q = pl.pallas_call(
        prepare_body,
        in_specs=[vmem] * 3 + [home],
        out_shape=(*[quarter] * 4, per_obs, *[shape((EXT, WIDE), F32)] * 5),
        scratch_shapes=[runs, pltpu.VMEM((EXT + ROWS + 10, LEV, WIDE), F32), sems((1,))],
        name="prepare",
        compiler_params=params(51.5),
    )(following, err, found, pack)

    gradient = pl.pallas_call(
        adjoint_body,
        in_specs=[vmem] * 13 + [home] * 3,
        out_shape=shape((fields, LON), F32),
        scratch_shapes=[
            pltpu.VMEM((PARTS * SENT, BLK), F32),
            pltpu.VMEM((4 * STEPS, LEV, HALF * BLK), F32),
            wide,
            wide,
            runs,
            field,
            field,
            field,
            sems((3,)),
        ],
        name="adjoint",
        compiler_params=params(51.45),
    )(arrived, previous, *put, *ahead, c, e, w, n, q, start, err, background.reshape(fields, LON))
    return (gradient.reshape(increments.shape), departures.reshape(values.shape))


def solution(mesh):
    in_specs = (
        P("tm", None, "space", None),
        P(None, "space", None),
        P(None, "space", None),
        P(None, "space", None),
        P("tm", None, "space", None, None),
        P("tm", None, "space", None),
        P("tm", None, "space", None),
        P("tm", None, "space", None),
        P("tm", None, "space"),
    )
    out_specs = (P("tm", None, "space", None), P("tm", None, "space", None))
    return jax.shard_map(local, mesh=mesh, in_specs=in_specs, out_specs=out_specs, check_vma=False)
```

```python
import jax
import jax.numpy as jnp
from jax import lax
from jax.experimental import pallas as pl
from jax.experimental.pallas import tpu as pltpu
from jax.sharding import PartitionSpec as P

LEV = 8
ROWS = 8
LON = 1440
WIDE = 1536
PAD = 48
STEPS = 4
HALO = 4
EXT = ROWS + 2 * HALO
FULL = 3 * ROWS
FIELD = LEV * ROWS
SENT_ROWS = FIELD + 4 * ROWS + LEV * HALO
OBS = 24
ALL_OBS = STEPS * OBS
BLK = 128
PARTS = 32
SLOTS = 2 * STEPS
SENT = 3 * SLOTS
HALF = 45
BLOCKS = 2 * HALF * LEV
F32 = jnp.float32
BF16 = jnp.bfloat16
I32 = jnp.int32


def iota(shape, dim):
    return lax.broadcasted_iota(I32, shape, dim)


def params(mib):
    return pltpu.CompilerParams(vmem_limit_bytes=int(mib * (1 << 20)))


def copies(sems, *pairs):
    found = [pltpu.make_async_copy(src, dst, sems.at[i]) for i, (src, dst) in enumerate(pairs)]
    for copy in found:
        copy.start()
    return found


def owner_rank(own_ref, step):
    sub, lane = iota((OBS, OBS), 0), iota((OBS, OBS), 1)
    across = jnp.broadcast_to(own_ref[step], (OBS, OBS)).astype(F32)
    down = jnp.sum(jnp.where(sub == lane, across, 0.0), axis=1, keepdims=True)
    same = down == across
    rank_across = jnp.sum(jnp.where(same & (sub < lane), 1.0, 0.0), axis=0, keepdims=True)
    rank_down = jnp.sum(jnp.where(same & (lane < sub), 1.0, 0.0), axis=1, keepdims=True)
    return down, across[:1], rank_down, rank_across


def request_body(own_hbm, col_hbm, _, out_ref, choice_ref, own_ref, col_ref, sems):
    for copy in copies(sems, (own_hbm, own_ref), (col_hbm, col_ref)):
        copy.wait()
    dest = iota((PARTS, OBS), 0).astype(F32)
    lane = iota((PARTS, BLK), 1)
    line = iota((PARTS, BLK), 0)
    from_lane = iota((OBS, PARTS * SLOTS), 1).astype(F32)
    asked = jnp.zeros((PARTS, BLK), F32)
    sends = [[], [], []]
    picks = []
    for step in range(STEPS):
        down, across, rank_down, rank_across = owner_rank(own_ref, step)
        block = col_ref[pl.ds(step, 1), :]
        group = (block * 1457) >> 16
        row = ((group & 1) * HALF + block - HALF * group) * LEV + (group >> 1)
        value = (row + 1).astype(F32)
        for nth in range(2):
            hit = (across == dest) & (rank_across == float(nth))
            found = jnp.sum(jnp.where(hit, value, 0.0), axis=1, keepdims=True)
            asked = jnp.where(lane == 2 * step + nth, found, asked)
        picks.append(jnp.where(from_lane == down * SLOTS + (2.0 * step) + rank_down, 1.0, 0.0))
        for side, shift in enumerate((0.0, 1.0, -1.0)):
            sends[side].append((across + shift) * SENT + (side * SLOTS + 2.0 * step) + rank_across)
    below = jnp.where(line == 0, 0.0, pltpu.roll(asked, 1, 0))
    above = jnp.where(line == PARTS - 1, 0.0, pltpu.roll(asked, PARTS - 1, 0))
    asked = asked + pltpu.roll(below, SLOTS, 1) + pltpu.roll(above, 2 * SLOTS, 1)
    out_ref[...] = asked.astype(I32) - 1
    pick = jnp.concatenate(picks, axis=0).astype(BF16)
    for half in range(2):
        choice_ref[pl.ds(PARTS * SENT + half * ALL_OBS, ALL_OBS), :] = pick[:, half * BLK : (half + 1) * BLK]
    spare = jnp.full((1, BLK - ALL_OBS), -1.0, F32)
    sends = [jnp.concatenate(parts + [spare], axis=1) for parts in sends]
    slot = iota((SLOTS, BLK), 0).astype(F32)
    for part in range(0, PARTS, 2):
        tiles = []
        for at in (part, part + 1):
            for side in range(3):
                tiles.append(jnp.where(sends[side] == slot + float(at * SENT + side * SLOTS), 1.0, 0.0))
        choice_ref[pl.ds(part * SENT, 2 * SENT), :] = jnp.concatenate(tiles, axis=0).astype(BF16)


def spread(tmp_ref, field):
    for run in range(LON // BLK):
        tmp_ref[run, : field.shape[0], :] = field[:, run * BLK : (run + 1) * BLK]
    tail = LON % BLK
    tmp_ref[LON // BLK, : field.shape[0], :] = jnp.concatenate(
        [field[:, LON - tail :], field[:, :PAD], field[:, LON - PAD :]], axis=1
    )


def spread_row(tmp_ref, row, apart=ROWS):
    return jnp.concatenate(
        [tmp_ref[run, pl.ds(row, LEV, stride=apart), :] for run in range(WIDE // BLK)], axis=1
    )


def put_row(tmp_ref, row, value):
    for run in range(WIDE // BLK):
        tmp_ref[run, pl.ds(row, LEV, stride=ROWS), :] = value[:, run * BLK : (run + 1) * BLK]


def gathered(tmp_ref):
    return jnp.concatenate([tmp_ref[run] for run in range(WIDE // BLK)], axis=1)[:, :LON]


def edges_body(inc_hbm, wts_hbm, err_hbm, val_hbm, wt_hbm, low_ref, high_ref, own_ref, aux_ref, err_ref, sems):
    for copy in copies(
        sems,
        (inc_hbm, own_ref.at[pl.ds(0, FIELD)]),
        (wts_hbm, own_ref.at[pl.ds(FIELD, 4 * ROWS)]),
        (err_hbm, err_ref),
        (val_hbm, aux_ref.at[pl.ds(0, ALL_OBS)]),
        (wt_hbm, aux_ref.at[pl.ds(ALL_OBS, ALL_OBS)]),
    ):
        copy.wait()
    both = own_ref[...].astype(BF16)
    for out_ref, first in ((low_ref, 0), (high_ref, HALO)):
        out_ref[0 : FIELD + 4 * ROWS, :] = both
        for level in range(0, LEV, 4):
            rows = [err_ref[(level + i) * ROWS + first : (level + i) * ROWS + first + HALO, :] for i in range(4)]
            at = FIELD + 4 * ROWS + level * HALO
            out_ref[at : at + 4 * HALO, :] = jnp.concatenate(rows, axis=0).astype(BF16)


def widen(value):
    tail = LON % BLK
    return jnp.concatenate(
        [value[:, : LON - tail], jnp.concatenate([value[:, LON - tail :], value[:, :PAD], value[:, LON - PAD :]], axis=1)],
        axis=1,
    )


def row_of(ref, which, row):
    return jnp.broadcast_to(ref[which, pl.ds(row, 1), :], (LEV, WIDE))


def forward_body(
    own_hbm, south_ref, north_ref, t1_ref, t2_ref, t3_ref, t4_ref, last_ref, next_ref, pack_ref,
    x_ref, flat_ref, wide_ref, low_tmp, own_tmp, high_tmp, own_ref, sems,
):
    (wait,) = copies(sems, (own_hbm, own_ref))
    spread(low_tmp, south_ref[FIELD + 4 * ROWS :, :].astype(F32))
    spread(high_tmp, north_ref[FIELD + 4 * ROWS :, :].astype(F32))
    for row in range(HALO):
        pack_ref[EXT + row] = spread_row(low_tmp, row, HALO)
        pack_ref[EXT + HALO + row] = spread_row(high_tmp, row, HALO)
    spread(low_tmp, south_ref[0:FIELD, :].astype(F32))
    spread(high_tmp, north_ref[0:FIELD, :].astype(F32))
    for row in range(ROWS):
        x_ref[row] = spread_row(low_tmp, row)
        x_ref[2 * ROWS + row] = spread_row(high_tmp, row)
    wait.wait()
    spread(own_tmp, own_ref[0:FIELD, :])
    for row in range(ROWS):
        x_ref[ROWS + row] = spread_row(own_tmp, row)
    for side in range(4):
        rows = slice(FIELD + side * ROWS, FIELD + (side + 1) * ROWS)
        for i, part_ref in enumerate((south_ref, own_ref, north_ref)):
            wide_ref[side + 1, i * ROWS : (i + 1) * ROWS, :] = widen(part_ref[rows, :].astype(F32))
    wide_ref[0] = 1.0 - (wide_ref[1] + wide_ref[2] + wide_ref[3] + wide_ref[4])
    for side in range(5):
        for half in range(2):
            first = HALO + half * ROWS
            pack_ref[EXT + ROWS + 2 * side + half] = wide_ref[side, first : first + ROWS, :]
    for row in range(0, EXT, 2):
        pair = [x_ref[HALO + row + i][:, :LON] for i in range(2)]
        next_ref[pl.ds(row * LEV, 2 * LEV), :] = jnp.concatenate(pair, axis=0).astype(BF16)

    for step in range(STEPS):
        old, new = (step % 2) * FULL, ((step + 1) % 2) * FULL
        for row in range(step + 1, FULL - step - 1):
            v = x_ref[old + row]
            moved = (
                row_of(wide_ref, 0, row) * v
                + row_of(wide_ref, 1, row) * pltpu.roll(v, WIDE - 1, 1)
                + row_of(wide_ref, 2, row) * pltpu.roll(v, 1, 1)
                + row_of(wide_ref, 3, row) * x_ref[old + row + 1]
                + row_of(wide_ref, 4, row) * x_ref[old + row - 1]
            )
            own = row - ROWS
            if step < STEPS - 1:
                x_ref[new + row] = moved
            else:
                pack_ref[row - HALO] = moved
                if 0 <= own < ROWS:
                    put_row(own_tmp, own, moved)
            if 0 <= own < ROWS:
                part = own % 4
                flat_ref[own // 4, :, part * LON : (part + 1) * LON] = moved[:, :LON]
        for pair in range(HALF):
            tiles = []
            for tile in (2 * pair, 2 * pair + 1):
                half, at = tile // HALF, tile % HALF
                tiles.append(flat_ref[half, :, at * BLK : (at + 1) * BLK])
            (t1_ref, t2_ref, t3_ref, t4_ref)[step][pl.ds(pair * 2 * LEV, 2 * LEV), :] = jnp.concatenate(tiles, axis=0).astype(BF16)
    last_ref[...] = gathered(own_tmp).astype(BF16)


def gather_body(asked_ref, t1_ref, t2_ref, t3_ref, t4_ref, out_ref, token_ref, slots_ref):
    lane = iota((PARTS, BLOCKS), 1)
    asked = asked_ref[...]
    for step in range(STEPS):
        picks = [
            jnp.where(asked[:, 2 * step + nth : 2 * step + nth + 1] == lane, 1.0, 0.0).astype(BF16)
            for nth in range(2)
        ]
        blocks = jnp.dot(jnp.concatenate(picks, axis=0), (t1_ref, t2_ref, t3_ref, t4_ref)[step][...], preferred_element_type=F32)
        for nth in range(2):
            slots_ref[pl.ds(2 * step + nth, PARTS, stride=SLOTS), :] = blocks[nth * PARTS : (nth + 1) * PARTS]
    out_ref[...] = slots_ref[...].astype(BF16)
    token_ref[...] = slots_ref[0:8, :]


def hold_body(token_ref, last_in, next_in, last_out, next_out, seen_ref):
    seen_ref[...] = token_ref[...]


def spread_out(block):
    line = iota(block.shape, 0)
    zero = jnp.zeros_like(block)
    return jnp.concatenate([jnp.where(line == i, block, zero) for i in range(block.shape[0])], axis=1)


GROUP = 16


def observe_body(
    got_ref, choice_hbm, aux_hbm, ops_hbm, _, dep_ref, out_ref, choice_ref, aux_ref, ops_ref, sems
):
    size = GROUP * BLK
    parts = [pl.ds(first, size) for first in range(0, ALL_OBS * BLK, size)]
    pairs = [(choice_hbm, choice_ref), (aux_hbm, aux_ref)]
    waits = copies(sems, *pairs, *[(ops_hbm.at[part], ops_ref.at[part]) for part in parts])
    waits[0].wait()
    base = PARTS * SENT
    pick = jnp.concatenate([choice_ref[base + half * ALL_OBS : base + (half + 1) * ALL_OBS, :] for half in range(2)], axis=1)
    seen = jnp.dot(pick, got_ref[...], preferred_element_type=F32).astype(BF16)
    waits[1].wait()
    line = iota((GROUP, BLK), 0)
    scaled = []
    for at in range(ALL_OBS // GROUP):
        waits[2 + at].wait()
        first = at * GROUP
        rows = slice(first, first + GROUP)
        product = jnp.zeros((GROUP, BLK), F32)
        for i in range(0, GROUP, 2):
            two = lax.dot_general(
                seen[rows],
                ops_ref[(first + i) * BLK : (first + i + 2) * BLK, :],
                (((1,), (1,)), ((), ())),
                preferred_element_type=F32,
            )
            product = jnp.where(line == i, two[:, :BLK], product)
            product = jnp.where(line == i + 1, two[:, BLK:], product)
        departure = product - aux_ref[first : first + GROUP, :]
        dep_ref[rows, :] = departure
        weight = aux_ref[ALL_OBS + first : ALL_OBS + first + GROUP, :]
        scaled.append((weight * departure).astype(BF16))
    steps = []
    for at, block in enumerate(scaled):
        first = at * GROUP
        steps.append(
            jnp.dot(
                spread_out(block), ops_ref[first * BLK : (first + GROUP) * BLK, :], preferred_element_type=F32
            ).astype(BF16)
        )
    increments = jnp.concatenate(steps, axis=0)
    out_ref[...] = jnp.dot(choice_ref[:base, :ALL_OBS], increments, preferred_element_type=F32).astype(BF16)


PAIRS = ((2, 3), (0, 1))
SIDES = ((0, 0, 0, BLOCKS), (1, BLOCKS, HALF * LEV, HALF * LEV), (2, BLOCKS + HALF * LEV, 0, HALF * LEV))


def put_body(asked_ref, late_ref, early_ref):
    asked = jnp.transpose(asked_ref[...].astype(F32))
    for at, steps in enumerate(PAIRS):
        for side, base, start, size in SIDES:
            named = jnp.concatenate(
                [asked[side * SLOTS + 2 * step + nth :][:1] for step in steps for nth in range(2)], axis=1
            )
            line = (iota((size, 4 * PARTS), 0) + start).astype(F32)
            (late_ref, early_ref)[at][base : base + size, :] = jnp.where(line == named, 1.0, 0.0).astype(BF16)


def prepare_body(
    next_ref, err_ref, pack_hbm, a_ref, b_ref, c_ref, d_ref, token_ref, *rest
):
    *coef_refs, own_tmp, pack_ref, sems = rest
    (wait,) = copies(sems, (pack_hbm, pack_ref))
    token_ref[...] = err_ref[:8, :BLK]
    spread(own_tmp, err_ref[...])
    wait.wait()
    final = lax.axis_index("tm") == lax.axis_size("tm") - 1
    for row in range(0, EXT, 2):
        both = next_ref[pl.ds(row * LEV, 2 * LEV), :].astype(F32)
        for i in range(2):
            at = row + i - HALO
            if 0 <= at < ROWS:
                weight = spread_row(own_tmp, at)
            else:
                weight = pack_ref[EXT + (row + i) % ROWS]
            ahead = weight * (pack_ref[row + i] - widen(both[i * LEV : (i + 1) * LEV]))
            (a_ref, b_ref, c_ref, d_ref)[row // 4][(row + i) % 4] = jnp.where(final, 0.0, ahead)
    for which, coef_ref in enumerate(coef_refs):
        for half in range(2):
            coef_ref[half * ROWS : (half + 1) * ROWS, :] = pack_ref[EXT + ROWS + 2 * which + half]


def adjoint_body(got_ref, prev_ref, late_ref, early_ref, *rest):
    first_refs, coef_refs = rest[:4], rest[4:9]
    inc_hbm, err_hbm, back_hbm, out_ref, got_f, flat_ref, a_ref, y_ref, tmp_ref, inc_ref, err_ref, back_ref, sems = rest[9:]
    waits = copies(sems, (inc_hbm, inc_ref), (err_hbm, err_ref), (back_hbm, back_ref))

    def weight(which, row):
        return jnp.broadcast_to(coef_refs[which][pl.ds(row, 1), :], (LEV, WIDE))

    got_f[...] = got_ref[...].astype(F32)
    for at, steps in enumerate(PAIRS):
        for side, base, start, size in SIDES:
            sides = []
            for i, step in enumerate(steps):
                terms = jnp.concatenate(
                    [got_f[pl.ds(side * SLOTS + 2 * step + nth, PARTS, stride=SENT), :] for nth in range(2)], axis=0
                ).astype(BF16)
                zero = jnp.zeros_like(terms)
                sides.append(jnp.concatenate([terms, zero] if i == 0 else [zero, terms], axis=0))
            added = jnp.dot(
                (late_ref, early_ref)[at][base : base + size, :],
                jnp.concatenate(sides, axis=1),
                preferred_element_type=F32
            )
            flat = (1, 0, 3)[side]
            for i, step in enumerate(steps):
                for tile in range(size // LEV):
                    half, run = tile // HALF, tile % HALF
                    flat_ref[step * 4 + flat + half, :, run * BLK : (run + 1) * BLK] = added[
                        tile * LEV : (tile + 1) * LEV, i * BLK : (i + 1) * BLK
                    ]
    for step in range(STEPS - 1, -1, -1):
        edge = STEPS - 1 - step
        for row in range(edge, EXT - edge):
            part = row % 4
            before = first_refs[row // 4][row % 4] if edge == 0 else y_ref[row]
            a_ref[row] = before + widen(flat_ref[step * 4 + row // 4, :, part * LON : (part + 1) * LON])
        for row in range(edge + 1, EXT - edge - 1):
            v = a_ref[row]
            pulled = (
                weight(0, row) * v
                + pltpu.roll(weight(1, row) * v, 1, 1)
                + pltpu.roll(weight(2, row) * v, WIDE - 1, 1)
                + weight(3, row - 1) * a_ref[row - 1]
                + weight(4, row + 1) * a_ref[row + 1]
            )
            if step:
                y_ref[row] = pulled
            else:
                put_row(tmp_ref, row - HALO, pulled)
    for wait in waits:
        wait.wait()
    begin = jnp.where(lax.axis_index("tm") == 0, back_ref[...], prev_ref[...].astype(F32))
    out_ref[...] = gathered(tmp_ref) + err_ref[...] * (inc_ref[...] - begin)


def shape(dims, dtype):
    return jax.ShapeDtypeStruct(dims, dtype)


def exchange(block):
    return lax.all_to_all(block, "space", split_axis=0, concat_axis=0, tiled=True)


def local(
    increments,
    background,
    error_weight,
    neighbor_weights,
    operators,
    values,
    obs_weight,
    owners,
    columns,
):
    fields = LEV * ROWS
    start = increments.reshape(fields, LON)
    owner = owners.reshape(STEPS, 1, OBS)
    windows, parts = lax.axis_size("tm"), lax.axis_size("space")
    vmem = pl.BlockSpec(memory_space=pltpu.VMEM)
    home = pl.BlockSpec(memory_space=pltpu.HBM)
    anywhere = pl.BlockSpec(memory_space=pl.ANY)
    sems = pltpu.SemaphoreType.DMA
    field = pltpu.VMEM((fields, LON), F32)
    runs = pltpu.VMEM((WIDE // BLK, fields, BLK), F32)
    wide = pltpu.VMEM((EXT, LEV, WIDE), F32)

    err = error_weight.reshape(fields, LON)
    stencil = neighbor_weights.reshape(4 * ROWS, LON)
    low, high, own, aux = pl.pallas_call(
        edges_body,
        in_specs=[home] * 5,
        out_shape=(
            shape((SENT_ROWS, LON), BF16),
            shape((SENT_ROWS, LON), BF16),
            shape((FIELD + 4 * ROWS, LON), F32),
            shape((2 * ALL_OBS, BLK), F32),
        ),
        scratch_shapes=[field, sems((5,))],
        name="edges",
        compiler_params=params(60),
    )(start, stencil, err, values.reshape(ALL_OBS, BLK), obs_weight.reshape(ALL_OBS, BLK))
    south = lax.ppermute(high, "space", [(i, i + 1) for i in range(parts - 1)])
    north = lax.ppermute(low, "space", [(i + 1, i) for i in range(parts - 1)])

    request, choice = pl.pallas_call(
        request_body,
        in_specs=[home, home, anywhere],
        out_shape=(
            shape((PARTS, BLK), I32),
            shape((PARTS * SENT + 2 * ALL_OBS, BLK), BF16),
        ),
        scratch_shapes=[pltpu.VMEM((STEPS, 1, OBS), I32), pltpu.VMEM((STEPS, OBS), I32), sems((2,))],
        name="request",
        compiler_params=params(60),
    )(owner, columns.reshape(STEPS, OBS), aux)
    asked = exchange(request)

    around = shape((EXT * LEV, LON), BF16)
    here = shape((fields, LON), BF16)
    *tables, last, following, pack = pl.pallas_call(
        forward_body,
        in_specs=[home, vmem, vmem],
        out_shape=(
            *[shape((BLOCKS, BLK), BF16) for _ in range(STEPS)],
            here,
            around,
            shape((EXT + ROWS + 10, LEV, WIDE), F32),
        ),
        scratch_shapes=[
            pltpu.VMEM((2 * FULL, LEV, WIDE), F32),
            pltpu.VMEM((2, LEV, HALF * BLK), F32),
            pltpu.VMEM((5, FULL, WIDE), F32),
            runs,
            runs,
            runs,
            pltpu.VMEM((FIELD + 4 * ROWS, LON), F32),
            sems((1,)),
        ],
        name="forward",
        compiler_params=params(51.45),
    )(own, south, north)

    mark = shape((8, BLK), F32)
    blocks, token = pl.pallas_call(
        gather_body,
        out_shape=(shape((PARTS * SLOTS, BLK), BF16), mark),
        scratch_shapes=[pltpu.VMEM((PARTS * SLOTS, BLK), F32)],
        name="gather",
        compiler_params=params(16),
    )(asked, *tables)
    got = exchange(blocks)

    last, following, token = pl.pallas_call(
        hold_body,
        in_specs=[vmem, anywhere, anywhere],
        out_specs=(anywhere, anywhere, vmem),
        out_shape=(here, around, mark),
        input_output_aliases={1: 0, 2: 1},
        name="hold",
        cost_estimate=pl.CostEstimate(flops=0, transcendentals=0, bytes_accessed=30_000_000),
        compiler_params=params(16),
    )(token, last, following)
    previous = lax.ppermute(last, "tm", [(i, i + 1) for i in range(windows - 1)])
    following = lax.ppermute(following, "tm", [(i + 1, i) for i in range(windows - 1)])

    quarter = shape((4, LEV, WIDE), F32)
    *ahead, token, c, e, w, n, q = pl.pallas_call(
        prepare_body,
        in_specs=[vmem] * 2 + [home],
        out_shape=(*[quarter] * 4, mark, *[shape((EXT, WIDE), F32)] * 5),
        scratch_shapes=[runs, pltpu.VMEM((EXT + ROWS + 10, LEV, WIDE), F32), sems((1,))],
        name="prepare",
        compiler_params=params(51.5),
    )(following, err, pack)

    per_obs = shape((ALL_OBS, BLK), F32)
    departures, slots = pl.pallas_call(
        observe_body,
        in_specs=[vmem] + [home] * 3 + [anywhere],
        out_shape=(per_obs, shape((PARTS * SENT, BLK), BF16)),
        scratch_shapes=[
            pltpu.VMEM((PARTS * SENT + 2 * ALL_OBS, BLK), BF16),
            pltpu.VMEM((2 * ALL_OBS, BLK), F32),
            pltpu.VMEM((ALL_OBS * BLK, BLK), BF16),
            sems((2 + ALL_OBS // GROUP,)),
        ],
        name="observe",
        compiler_params=params(53.78),
    )(got, choice, aux, operators.reshape(ALL_OBS * BLK, BLK), token)
    arrived = exchange(slots)

    half = shape((2 * BLOCKS, BLK), BF16)
    put = pl.pallas_call(put_body, out_shape=(half, half), name="put", compiler_params=params(16))(asked)
    gradient = pl.pallas_call(
        adjoint_body,
        in_specs=[vmem] * 13 + [home] * 3,
        out_shape=shape((fields, LON), F32),
        scratch_shapes=[
            pltpu.VMEM((PARTS * SENT, BLK), F32),
            pltpu.VMEM((4 * STEPS, LEV, HALF * BLK), F32),
            wide,
            wide,
            runs,
            field,
            field,
            field,
            sems((3,)),
        ],
        name="adjoint",
        compiler_params=params(51.45),
    )(arrived, previous, *put, *ahead, c, e, w, n, q, start, err, background.reshape(fields, LON))
    return (gradient.reshape(increments.shape), departures.reshape(values.shape))


def solution(mesh):
    in_specs = (
        P("tm", None, "space", None),
        P(None, "space", None),
        P(None, "space", None),
        P(None, "space", None),
        P("tm", None, "space", None, None),
        P("tm", None, "space", None),
        P("tm", None, "space", None),
        P("tm", None, "space", None),
        P("tm", None, "space"),
    )
    out_specs = (P("tm", None, "space", None), P("tm", None, "space", None))
    return jax.shard_map(local, mesh=mesh, in_specs=in_specs, out_specs=out_specs, check_vma=False)
```

```python
import jax
import jax.numpy as jnp
from jax import lax
from jax.experimental import pallas as pl
from jax.experimental.pallas import tpu as pltpu
from jax.sharding import PartitionSpec as P

LEV = 8
ROWS = 8
LON = 1440
WIDE = 1536
PAD = 48
STEPS = 4
HALO = 4
EXT = ROWS + 2 * HALO
FULL = 3 * ROWS
FIELD = LEV * ROWS
SENT_ROWS = FIELD + 4 * ROWS + LEV * HALO
OBS = 24
ALL_OBS = STEPS * OBS
BLK = 128
PARTS = 32
SLOTS = 2 * STEPS
SENT = 3 * SLOTS
HALF = 45
BLOCKS = 2 * HALF * LEV
F32 = jnp.float32
BF16 = jnp.bfloat16
I32 = jnp.int32


def iota(shape, dim):
    return lax.broadcasted_iota(I32, shape, dim)


def params(mib):
    return pltpu.CompilerParams(vmem_limit_bytes=int(mib * (1 << 20)))


def copies(sems, *pairs):
    found = [pltpu.make_async_copy(src, dst, sems.at[i]) for i, (src, dst) in enumerate(pairs)]
    for copy in found:
        copy.start()
    return found


def owner_rank(own_ref, step):
    sub, lane = iota((OBS, OBS), 0), iota((OBS, OBS), 1)
    across = jnp.broadcast_to(own_ref[step], (OBS, OBS)).astype(F32)
    down = jnp.sum(jnp.where(sub == lane, across, 0.0), axis=1, keepdims=True)
    same = down == across
    rank_across = jnp.sum(jnp.where(same & (sub < lane), 1.0, 0.0), axis=0, keepdims=True)
    rank_down = jnp.sum(jnp.where(same & (lane < sub), 1.0, 0.0), axis=1, keepdims=True)
    return down, across[:1], rank_down, rank_across


def request_body(own_hbm, col_hbm, _, out_ref, choice_ref, own_ref, col_ref, sems):
    for copy in copies(sems, (own_hbm, own_ref), (col_hbm, col_ref)):
        copy.wait()
    dest = iota((PARTS, OBS), 0).astype(F32)
    lane = iota((PARTS, BLK), 1)
    line = iota((PARTS, BLK), 0)
    from_lane = iota((OBS, PARTS * SLOTS), 1).astype(F32)
    asked = jnp.zeros((PARTS, BLK), F32)
    sends = [[], [], []]
    picks = []
    for step in range(STEPS):
        down, across, rank_down, rank_across = owner_rank(own_ref, step)
        block = col_ref[pl.ds(step, 1), :]
        group = (block * 1457) >> 16
        row = ((group & 1) * HALF + block - HALF * group) * LEV + (group >> 1)
        value = (row + 1).astype(F32)
        for nth in range(2):
            hit = (across == dest) & (rank_across == float(nth))
            found = jnp.sum(jnp.where(hit, value, 0.0), axis=1, keepdims=True)
            asked = jnp.where(lane == 2 * step + nth, found, asked)
        picks.append(jnp.where(from_lane == down * SLOTS + (2.0 * step) + rank_down, 1.0, 0.0))
        for side, shift in enumerate((0.0, 1.0, -1.0)):
            sends[side].append((across + shift) * SENT + (side * SLOTS + 2.0 * step) + rank_across)
    below = jnp.where(line == 0, 0.0, pltpu.roll(asked, 1, 0))
    above = jnp.where(line == PARTS - 1, 0.0, pltpu.roll(asked, PARTS - 1, 0))
    asked = asked + pltpu.roll(below, SLOTS, 1) + pltpu.roll(above, 2 * SLOTS, 1)
    out_ref[...] = asked.astype(I32) - 1
    pick = jnp.concatenate(picks, axis=0).astype(BF16)
    for half in range(2):
        choice_ref[pl.ds(PARTS * SENT + half * ALL_OBS, ALL_OBS), :] = pick[:, half * BLK : (half + 1) * BLK]
    spare = jnp.full((1, BLK - ALL_OBS), -1.0, F32)
    sends = [jnp.concatenate(parts + [spare], axis=1) for parts in sends]
    slot = iota((SLOTS, BLK), 0).astype(F32)
    for part in range(0, PARTS, 2):
        tiles = []
        for at in (part, part + 1):
            for side in range(3):
                tiles.append(jnp.where(sends[side] == slot + float(at * SENT + side * SLOTS), 1.0, 0.0))
        choice_ref[pl.ds(part * SENT, 2 * SENT), :] = jnp.concatenate(tiles, axis=0).astype(BF16)


def spread(tmp_ref, field):
    for run in range(LON // BLK):
        tmp_ref[run, : field.shape[0], :] = field[:, run * BLK : (run + 1) * BLK]
    tail = LON % BLK
    tmp_ref[LON // BLK, : field.shape[0], :] = jnp.concatenate(
        [field[:, LON - tail :], field[:, :PAD], field[:, LON - PAD :]], axis=1
    )


def spread_row(tmp_ref, row, apart=ROWS):
    return jnp.concatenate(
        [tmp_ref[run, pl.ds(row, LEV, stride=apart), :] for run in range(WIDE // BLK)], axis=1
    )


def put_row(tmp_ref, row, value):
    for run in range(WIDE // BLK):
        tmp_ref[run, pl.ds(row, LEV, stride=ROWS), :] = value[:, run * BLK : (run + 1) * BLK]


def gathered(tmp_ref):
    return jnp.concatenate([tmp_ref[run] for run in range(WIDE // BLK)], axis=1)[:, :LON]


def edges_body(inc_hbm, wts_hbm, err_hbm, val_hbm, wt_hbm, low_ref, high_ref, own_ref, aux_ref, err_ref, sems):
    for copy in copies(
        sems,
        (inc_hbm, own_ref.at[pl.ds(0, FIELD)]),
        (wts_hbm, own_ref.at[pl.ds(FIELD, 4 * ROWS)]),
        (err_hbm, err_ref),
        (val_hbm, aux_ref.at[pl.ds(0, ALL_OBS)]),
        (wt_hbm, aux_ref.at[pl.ds(ALL_OBS, ALL_OBS)]),
    ):
        copy.wait()
    both = own_ref[...].astype(BF16)
    for out_ref, first in ((low_ref, 0), (high_ref, HALO)):
        out_ref[0 : FIELD + 4 * ROWS, :] = both
        for level in range(0, LEV, 4):
            rows = [err_ref[(level + i) * ROWS + first : (level + i) * ROWS + first + HALO, :] for i in range(4)]
            at = FIELD + 4 * ROWS + level * HALO
            out_ref[at : at + 4 * HALO, :] = jnp.concatenate(rows, axis=0).astype(BF16)


def widen(value):
    tail = LON % BLK
    return jnp.concatenate(
        [value[:, : LON - tail], jnp.concatenate([value[:, LON - tail :], value[:, :PAD], value[:, LON - PAD :]], axis=1)],
        axis=1,
    )


def row_of(ref, which, row):
    return jnp.broadcast_to(ref[which, pl.ds(row, 1), :], (LEV, WIDE))


def forward_body(
    own_hbm, south_ref, north_ref, t1_ref, t2_ref, t3_ref, t4_ref, last_ref, next_ref, pack_ref,
    x_ref, flat_ref, wide_ref, low_tmp, own_tmp, high_tmp, own_ref, sems,
):
    (wait,) = copies(sems, (own_hbm, own_ref))
    spread(low_tmp, south_ref[FIELD + 4 * ROWS :, :].astype(F32))
    spread(high_tmp, north_ref[FIELD + 4 * ROWS :, :].astype(F32))
    for row in range(HALO):
        pack_ref[EXT + row] = spread_row(low_tmp, row, HALO)
        pack_ref[EXT + HALO + row] = spread_row(high_tmp, row, HALO)
    spread(low_tmp, south_ref[0:FIELD, :].astype(F32))
    spread(high_tmp, north_ref[0:FIELD, :].astype(F32))
    for row in range(ROWS):
        x_ref[row] = spread_row(low_tmp, row)
        x_ref[2 * ROWS + row] = spread_row(high_tmp, row)
    wait.wait()
    spread(own_tmp, own_ref[0:FIELD, :])
    for row in range(ROWS):
        x_ref[ROWS + row] = spread_row(own_tmp, row)
    for side in range(4):
        rows = slice(FIELD + side * ROWS, FIELD + (side + 1) * ROWS)
        for i, part_ref in enumerate((south_ref, own_ref, north_ref)):
            wide_ref[side + 1, i * ROWS : (i + 1) * ROWS, :] = widen(part_ref[rows, :].astype(F32))
    wide_ref[0] = 1.0 - (wide_ref[1] + wide_ref[2] + wide_ref[3] + wide_ref[4])
    for side in range(5):
        for half in range(2):
            first = HALO + half * ROWS
            pack_ref[EXT + ROWS + 2 * side + half] = wide_ref[side, first : first + ROWS, :]
    for row in range(0, EXT, 2):
        pair = [x_ref[HALO + row + i][:, :LON] for i in range(2)]
        next_ref[pl.ds(row * LEV, 2 * LEV), :] = jnp.concatenate(pair, axis=0).astype(BF16)

    for step in range(STEPS):
        old, new = (step % 2) * FULL, ((step + 1) % 2) * FULL
        for row in range(step + 1, FULL - step - 1):
            v = x_ref[old + row]
            moved = (
                row_of(wide_ref, 0, row) * v
                + row_of(wide_ref, 1, row) * pltpu.roll(v, WIDE - 1, 1)
                + row_of(wide_ref, 2, row) * pltpu.roll(v, 1, 1)
                + row_of(wide_ref, 3, row) * x_ref[old + row + 1]
                + row_of(wide_ref, 4, row) * x_ref[old + row - 1]
            )
            own = row - ROWS
            if step < STEPS - 1:
                x_ref[new + row] = moved
            else:
                pack_ref[row - HALO] = moved
                if 0 <= own < ROWS:
                    put_row(own_tmp, own, moved)
            if 0 <= own < ROWS:
                part = own % 4
                flat_ref[own // 4, :, part * LON : (part + 1) * LON] = moved[:, :LON]
        for pair in range(HALF):
            tiles = []
            for tile in (2 * pair, 2 * pair + 1):
                half, at = tile // HALF, tile % HALF
                tiles.append(flat_ref[half, :, at * BLK : (at + 1) * BLK])
            (t1_ref, t2_ref, t3_ref, t4_ref)[step][pl.ds(pair * 2 * LEV, 2 * LEV), :] = jnp.concatenate(tiles, axis=0).astype(BF16)
    last_ref[...] = gathered(own_tmp).astype(BF16)


def gather_body(asked_ref, t1_ref, t2_ref, t3_ref, t4_ref, last_in, next_in, out_ref, last_out, next_out, slots_ref):
    lane = iota((PARTS, BLOCKS), 1)
    asked = asked_ref[...]
    for step in range(STEPS):
        picks = [
            jnp.where(asked[:, 2 * step + nth : 2 * step + nth + 1] == lane, 1.0, 0.0).astype(BF16)
            for nth in range(2)
        ]
        blocks = jnp.dot(jnp.concatenate(picks, axis=0), (t1_ref, t2_ref, t3_ref, t4_ref)[step][...], preferred_element_type=F32)
        for nth in range(2):
            slots_ref[pl.ds(2 * step + nth, PARTS, stride=SLOTS), :] = blocks[nth * PARTS : (nth + 1) * PARTS]
    out_ref[...] = slots_ref[...].astype(BF16)


def spread_out(block):
    line = iota(block.shape, 0)
    zero = jnp.zeros_like(block)
    return jnp.concatenate([jnp.where(line == i, block, zero) for i in range(block.shape[0])], axis=1)


GROUP = 16


def observe_body(
    got_ref, choice_hbm, aux_hbm, ops_hbm, _, dep_ref, out_ref, choice_ref, aux_ref, ops_ref, sems
):
    size = GROUP * BLK
    parts = [pl.ds(first, size) for first in range(0, ALL_OBS * BLK, size)]
    pairs = [(choice_hbm, choice_ref), (aux_hbm, aux_ref)]
    waits = copies(sems, *pairs, *[(ops_hbm.at[part], ops_ref.at[part]) for part in parts])
    waits[0].wait()
    base = PARTS * SENT
    pick = jnp.concatenate([choice_ref[base + half * ALL_OBS : base + (half + 1) * ALL_OBS, :] for half in range(2)], axis=1)
    seen = jnp.dot(pick, got_ref[...], preferred_element_type=F32).astype(BF16)
    waits[1].wait()
    line = iota((GROUP, BLK), 0)
    scaled = []
    for at in range(ALL_OBS // GROUP):
        waits[2 + at].wait()
        first = at * GROUP
        rows = slice(first, first + GROUP)
        product = jnp.zeros((GROUP, BLK), F32)
        for i in range(0, GROUP, 2):
            two = lax.dot_general(
                seen[rows],
                ops_ref[(first + i) * BLK : (first + i + 2) * BLK, :],
                (((1,), (1,)), ((), ())),
                preferred_element_type=F32,
            )
            product = jnp.where(line == i, two[:, :BLK], product)
            product = jnp.where(line == i + 1, two[:, BLK:], product)
        departure = product - aux_ref[first : first + GROUP, :]
        dep_ref[rows, :] = departure
        weight = aux_ref[ALL_OBS + first : ALL_OBS + first + GROUP, :]
        scaled.append((weight * departure).astype(BF16))
    steps = []
    for at, block in enumerate(scaled):
        first = at * GROUP
        steps.append(
            jnp.dot(
                spread_out(block), ops_ref[first * BLK : (first + GROUP) * BLK, :], preferred_element_type=F32
            ).astype(BF16)
        )
    increments = jnp.concatenate(steps, axis=0)
    out_ref[...] = jnp.dot(choice_ref[:base, :ALL_OBS], increments, preferred_element_type=F32).astype(BF16)


PAIRS = ((2, 3), (0, 1))
SIDES = ((0, 0, 0, BLOCKS), (1, BLOCKS, HALF * LEV, HALF * LEV), (2, BLOCKS + HALF * LEV, 0, HALF * LEV))


def put_body(asked_ref, late_ref, early_ref):
    asked = jnp.transpose(asked_ref[...].astype(F32))
    for at, steps in enumerate(PAIRS):
        for side, base, start, size in SIDES:
            named = jnp.concatenate(
                [asked[side * SLOTS + 2 * step + nth :][:1] for step in steps for nth in range(2)], axis=1
            )
            line = (iota((size, 4 * PARTS), 0) + start).astype(F32)
            (late_ref, early_ref)[at][base : base + size, :] = jnp.where(line == named, 1.0, 0.0).astype(BF16)


def prepare_body(
    next_ref, err_ref, pack_hbm, a_ref, b_ref, c_ref, d_ref, token_ref, *rest
):
    *coef_refs, own_tmp, pack_ref, sems = rest
    (wait,) = copies(sems, (pack_hbm, pack_ref))
    token_ref[...] = err_ref[:8, :BLK]
    spread(own_tmp, err_ref[...])
    wait.wait()
    final = lax.axis_index("tm") == lax.axis_size("tm") - 1
    for row in range(0, EXT, 2):
        both = next_ref[pl.ds(row * LEV, 2 * LEV), :].astype(F32)
        for i in range(2):
            at = row + i - HALO
            if 0 <= at < ROWS:
                weight = spread_row(own_tmp, at)
            else:
                weight = pack_ref[EXT + (row + i) % ROWS]
            ahead = weight * (pack_ref[row + i] - widen(both[i * LEV : (i + 1) * LEV]))
            (a_ref, b_ref, c_ref, d_ref)[row // 4][(row + i) % 4] = jnp.where(final, 0.0, ahead)
    for which, coef_ref in enumerate(coef_refs):
        for half in range(2):
            coef_ref[half * ROWS : (half + 1) * ROWS, :] = pack_ref[EXT + ROWS + 2 * which + half]


def adjoint_body(got_ref, prev_ref, late_ref, early_ref, *rest):
    first_refs, coef_refs = rest[:4], rest[4:9]
    inc_hbm, err_hbm, back_hbm, out_ref, got_f, flat_ref, a_ref, y_ref, tmp_ref, inc_ref, err_ref, back_ref, sems = rest[9:]
    waits = copies(sems, (inc_hbm, inc_ref), (err_hbm, err_ref), (back_hbm, back_ref))

    def weight(which, row):
        return jnp.broadcast_to(coef_refs[which][pl.ds(row, 1), :], (LEV, WIDE))

    got_f[...] = got_ref[...].astype(F32)
    for at, steps in enumerate(PAIRS):
        for side, base, start, size in SIDES:
            sides = []
            for i, step in enumerate(steps):
                terms = jnp.concatenate(
                    [got_f[pl.ds(side * SLOTS + 2 * step + nth, PARTS, stride=SENT), :] for nth in range(2)], axis=0
                ).astype(BF16)
                zero = jnp.zeros_like(terms)
                sides.append(jnp.concatenate([terms, zero] if i == 0 else [zero, terms], axis=0))
            added = jnp.dot(
                (late_ref, early_ref)[at][base : base + size, :],
                jnp.concatenate(sides, axis=1),
                preferred_element_type=F32
            )
            flat = (1, 0, 3)[side]
            for i, step in enumerate(steps):
                for tile in range(size // LEV):
                    half, run = tile // HALF, tile % HALF
                    flat_ref[step * 4 + flat + half, :, run * BLK : (run + 1) * BLK] = added[
                        tile * LEV : (tile + 1) * LEV, i * BLK : (i + 1) * BLK
                    ]
    for step in range(STEPS - 1, -1, -1):
        edge = STEPS - 1 - step
        for row in range(edge, EXT - edge):
            part = row % 4
            before = first_refs[row // 4][row % 4] if edge == 0 else y_ref[row]
            a_ref[row] = before + widen(flat_ref[step * 4 + row // 4, :, part * LON : (part + 1) * LON])
        for row in range(edge + 1, EXT - edge - 1):
            v = a_ref[row]
            pulled = (
                weight(0, row) * v
                + pltpu.roll(weight(1, row) * v, 1, 1)
                + pltpu.roll(weight(2, row) * v, WIDE - 1, 1)
                + weight(3, row - 1) * a_ref[row - 1]
                + weight(4, row + 1) * a_ref[row + 1]
            )
            if step:
                y_ref[row] = pulled
            else:
                put_row(tmp_ref, row - HALO, pulled)
    for wait in waits:
        wait.wait()
    begin = jnp.where(lax.axis_index("tm") == 0, back_ref[...], prev_ref[...].astype(F32))
    out_ref[...] = gathered(tmp_ref) + err_ref[...] * (inc_ref[...] - begin)


def shape(dims, dtype):
    return jax.ShapeDtypeStruct(dims, dtype)


def exchange(block):
    return lax.all_to_all(block, "space", split_axis=0, concat_axis=0, tiled=True)


def local(
    increments,
    background,
    error_weight,
    neighbor_weights,
    operators,
    values,
    obs_weight,
    owners,
    columns,
):
    fields = LEV * ROWS
    start = increments.reshape(fields, LON)
    owner = owners.reshape(STEPS, 1, OBS)
    windows, parts = lax.axis_size("tm"), lax.axis_size("space")
    vmem = pl.BlockSpec(memory_space=pltpu.VMEM)
    home = pl.BlockSpec(memory_space=pltpu.HBM)
    anywhere = pl.BlockSpec(memory_space=pl.ANY)
    sems = pltpu.SemaphoreType.DMA
    field = pltpu.VMEM((fields, LON), F32)
    runs = pltpu.VMEM((WIDE // BLK, fields, BLK), F32)
    wide = pltpu.VMEM((EXT, LEV, WIDE), F32)

    err = error_weight.reshape(fields, LON)
    stencil = neighbor_weights.reshape(4 * ROWS, LON)
    low, high, own, aux = pl.pallas_call(
        edges_body,
        in_specs=[home] * 5,
        out_shape=(
            shape((SENT_ROWS, LON), BF16),
            shape((SENT_ROWS, LON), BF16),
            shape((FIELD + 4 * ROWS, LON), F32),
            shape((2 * ALL_OBS, BLK), F32),
        ),
        scratch_shapes=[field, sems((5,))],
        name="edges",
        compiler_params=params(60),
    )(start, stencil, err, values.reshape(ALL_OBS, BLK), obs_weight.reshape(ALL_OBS, BLK))
    south = lax.ppermute(high, "space", [(i, i + 1) for i in range(parts - 1)])
    north = lax.ppermute(low, "space", [(i + 1, i) for i in range(parts - 1)])

    request, choice = pl.pallas_call(
        request_body,
        in_specs=[home, home, anywhere],
        out_shape=(
            shape((PARTS, BLK), I32),
            shape((PARTS * SENT + 2 * ALL_OBS, BLK), BF16),
        ),
        scratch_shapes=[pltpu.VMEM((STEPS, 1, OBS), I32), pltpu.VMEM((STEPS, OBS), I32), sems((2,))],
        name="request",
        compiler_params=params(60),
    )(owner, columns.reshape(STEPS, OBS), aux)
    asked = exchange(request)

    around = shape((EXT * LEV, LON), BF16)
    here = shape((fields, LON), BF16)
    *tables, last, following, pack = pl.pallas_call(
        forward_body,
        in_specs=[home, vmem, vmem],
        out_shape=(
            *[shape((BLOCKS, BLK), BF16) for _ in range(STEPS)],
            here,
            around,
            shape((EXT + ROWS + 10, LEV, WIDE), F32),
        ),
        scratch_shapes=[
            pltpu.VMEM((2 * FULL, LEV, WIDE), F32),
            pltpu.VMEM((2, LEV, HALF * BLK), F32),
            pltpu.VMEM((5, FULL, WIDE), F32),
            runs,
            runs,
            runs,
            pltpu.VMEM((FIELD + 4 * ROWS, LON), F32),
            sems((1,)),
        ],
        name="forward",
        compiler_params=params(51.45),
    )(own, south, north)

    mark = shape((8, BLK), F32)
    blocks, last, following = pl.pallas_call(
        gather_body,
        in_specs=[vmem] * 5 + [anywhere] * 2,
        out_specs=(vmem, anywhere, anywhere),
        out_shape=(shape((PARTS * SLOTS, BLK), BF16), here, around),
        input_output_aliases={5: 1, 6: 2},
        scratch_shapes=[pltpu.VMEM((PARTS * SLOTS, BLK), F32)],
        name="gather",
        compiler_params=params(16),
    )(asked, *tables, last, following)
    got = exchange(blocks)

    previous = lax.ppermute(last, "tm", [(i, i + 1) for i in range(windows - 1)])
    following = lax.ppermute(following, "tm", [(i + 1, i) for i in range(windows - 1)])

    quarter = shape((4, LEV, WIDE), F32)
    *ahead, token, c, e, w, n, q = pl.pallas_call(
        prepare_body,
        in_specs=[vmem] * 2 + [home],
        out_shape=(*[quarter] * 4, mark, *[shape((EXT, WIDE), F32)] * 5),
        scratch_shapes=[runs, pltpu.VMEM((EXT + ROWS + 10, LEV, WIDE), F32), sems((1,))],
        name="prepare",
        compiler_params=params(51.5),
    )(following, err, pack)

    per_obs = shape((ALL_OBS, BLK), F32)
    departures, slots = pl.pallas_call(
        observe_body,
        in_specs=[vmem] + [home] * 3 + [anywhere],
        out_shape=(per_obs, shape((PARTS * SENT, BLK), BF16)),
        scratch_shapes=[
            pltpu.VMEM((PARTS * SENT + 2 * ALL_OBS, BLK), BF16),
            pltpu.VMEM((2 * ALL_OBS, BLK), F32),
            pltpu.VMEM((ALL_OBS * BLK, BLK), BF16),
            sems((2 + ALL_OBS // GROUP,)),
        ],
        name="observe",
        compiler_params=params(53.78),
    )(got, choice, aux, operators.reshape(ALL_OBS * BLK, BLK), token)
    arrived = exchange(slots)

    half = shape((2 * BLOCKS, BLK), BF16)
    put = pl.pallas_call(put_body, out_shape=(half, half), name="put", compiler_params=params(16))(asked)
    gradient = pl.pallas_call(
        adjoint_body,
        in_specs=[vmem] * 13 + [home] * 3,
        out_shape=shape((fields, LON), F32),
        scratch_shapes=[
            pltpu.VMEM((PARTS * SENT, BLK), F32),
            pltpu.VMEM((4 * STEPS, LEV, HALF * BLK), F32),
            wide,
            wide,
            runs,
            field,
            field,
            field,
            sems((3,)),
        ],
        name="adjoint",
        compiler_params=params(51.45),
    )(arrived, previous, *put, *ahead, c, e, w, n, q, start, err, background.reshape(fields, LON))
    return (gradient.reshape(increments.shape), departures.reshape(values.shape))


def solution(mesh):
    in_specs = (
        P("tm", None, "space", None),
        P(None, "space", None),
        P(None, "space", None),
        P(None, "space", None),
        P("tm", None, "space", None, None),
        P("tm", None, "space", None),
        P("tm", None, "space", None),
        P("tm", None, "space", None),
        P("tm", None, "space"),
    )
    out_specs = (P("tm", None, "space", None), P("tm", None, "space", None))
    return jax.shard_map(local, mesh=mesh, in_specs=in_specs, out_specs=out_specs, check_vma=False)
```
